512 devices in a mesh: prow: 32 (over z, core), pcol: 16 (over x, y).
Axes of the slice: x: 4, y: 4, z: 16, core: 2. Of those that a mesh axis runs over, the one named last changes fastest.
Arguments:
- trailing: bfloat16 [8, 8192, 2, 4096], P(None, 'prow', None, 'pcol'), may hold values from -6 to 6
- panel: bfloat16 [256, 8, 8192], P('pcol', None, 'prow'), may hold values from -1 to 1
- lower_inverse: bfloat16 [256, 256], replicated
- upper_inverse: bfloat16 [256, 256], replicated
- pivots: int32 [256], replicated, may hold values from 0 to 65535, as said below
Outputs:
- updated: bfloat16 [8, 8192, 2, 4096], P(None, 'prow', None, 'pcol')
The draws below stay inside these ranges and needn't reach their ends.
Inputs may be any that keep to these rules, and one draw needn't show every extreme that they name: `pivots`: the entries are distinct; entry i is either i or a row index of 256 or more. Entry 0 is 0 and entry 1 is 65535.
All inputs are finite; a program needn't handle non-finite values.
Results may differ from the reference program's by a relative error of at most 0.0054.
Values may be sent and summed in bfloat16 or wider, within the bound.
A program may use at most 64 MiB of HBM per device.

```python
import jax
import jax.numpy as jnp
from jax import lax

NB = 256
RB_DEV = 8
CB_DEV = 2
ROWS = 65536
COLS = 8192
N_PROW = 32
N_PCOL = 16


def draw_pivots(key, part):
    key_rows = jax.random.fold_in(key, 11)
    key_stay = jax.random.fold_in(key, 12)
    targets = jax.random.permutation(key_rows, ROWS - NB - 1)[:NB].astype(jnp.int32) + NB
    targets = targets.at[1].set(ROWS - 1)
    stays = jax.random.randint(key_stay, (NB,), 0, 8) == 0
    stays = stays.at[0].set(True).at[1].set(False)
    return jnp.where(stays, jnp.arange(NB, dtype=jnp.int32), targets)


def draw_lower_inverse(key, part):
    row_ids = jnp.arange(NB)[:, None]
    col_ids = jnp.arange(NB)[None, :]
    key_noise = jax.random.fold_in(key, 21)
    noise = jax.random.normal(key_noise, (NB, NB), jnp.float32)
    spread = 1.0 / NB ** 0.5
    values = jnp.where(row_ids > col_ids, noise * spread, jnp.where(row_ids == col_ids, 1.0, 0.0))
    return values.astype(jnp.float32).astype(jnp.bfloat16)


def draw_upper_inverse(key, part):
    row_ids = jnp.arange(NB)[:, None]
    col_ids = jnp.arange(NB)[None, :]
    key_noise = jax.random.fold_in(key, 31)
    key_diag = jax.random.fold_in(key, 32)
    noise = jax.random.normal(key_noise, (NB, NB), jnp.float32)
    diagonal = jnp.exp(jax.random.uniform(key_diag, (NB, NB), jnp.float32, -0.7, 0.7))
    spread = 1.0 / NB ** 0.5
    values = jnp.where(row_ids < col_ids, noise * spread, jnp.where(row_ids == col_ids, diagonal, 0.0))
    return values.astype(jnp.float32).astype(jnp.bfloat16)


def shard_levels(rng, dims, shards, smallest, high):
    level, own = 1.0, jax.random.fold_in(rng, 6)
    for position, blocks in shards:
        heights = jnp.exp(jax.random.uniform(jax.random.fold_in(own, position), (blocks,), jnp.float32, smallest / len(shards), high / len(shards)))
        level = level * jnp.repeat(heights, dims[position] // blocks).reshape([-1 if axis == position else 1 for axis in range(len(dims))])
    return level


def bell_draw(own_key, dims, width, limit, pieces=(), held_as=jnp.bfloat16):
    loudness = shard_levels(own_key, dims, pieces, -0.22, 0.18) if pieces else 1.0
    drawn = jax.random.normal(own_key, dims, jnp.float32) * width * loudness
    return jnp.minimum(jnp.maximum(drawn, -limit), limit).astype(held_as)


def setup_inputs(seed: int = 0) -> dict:
    key_list = jax.random.split(jax.random.key(seed), 6)
    trailing = bell_draw(key_list[0], (RB_DEV, N_PROW * NB, CB_DEV, N_PCOL * NB), 1.0, 6.0, ((1, 32), (3, 16)))
    panel = bell_draw(key_list[1], (NB, RB_DEV, N_PROW * NB), 0.0625, 1.0, ((0, 16), (2, 32)))
    lower_inverse = draw_lower_inverse(jax.random.fold_in(key_list[5], 71), 0)
    upper_inverse = draw_upper_inverse(jax.random.fold_in(key_list[5], 71), 0)
    pivots = draw_pivots(jax.random.fold_in(key_list[5], 71), 0)
    return {"trailing": trailing, "panel": panel, "lower_inverse": lower_inverse, "upper_inverse": upper_inverse, "pivots": pivots}


def reference(trailing, panel, lower_inverse, upper_inverse, pivots):
    matrix = trailing.reshape(ROWS, COLS)
    panel_t = panel.reshape(NB, ROWS)
    head_rows = jnp.arange(NB, dtype=jnp.int32)
    is_moved = pivots != head_rows
    row_order = jnp.arange(ROWS, dtype=jnp.int32)
    row_order = row_order.at[head_rows].set(pivots.astype(jnp.int32))
    row_order = row_order.at[jnp.where(is_moved, pivots, head_rows).astype(jnp.int32)].set(head_rows)
    top_rows = jnp.take(matrix, row_order[:NB], axis=0)
    top_solved = jnp.dot(lower_inverse, top_rows, preferred_element_type=jnp.float32).astype(jnp.bfloat16)
    lower_t = jnp.dot(upper_inverse.T, panel_t, preferred_element_type=jnp.float32).astype(jnp.bfloat16)
    lower_rows = lower_t.T.reshape(ROWS // NB, NB, NB)
    order_blocks = row_order.reshape(ROWS // NB, NB)

    def update_block(pair):
        block_ids, lower_block = pair
        rows_block = jnp.take(matrix, block_ids, axis=0)
        product = jnp.dot(lower_block, top_solved, preferred_element_type=jnp.float32)
        return (rows_block.astype(jnp.float32) - product).astype(jnp.bfloat16)

    updated = lax.map(update_block, (order_blocks, lower_rows))
    updated = updated.at[0].set(top_solved)
    return updated.reshape(RB_DEV, N_PROW * NB, CB_DEV, N_PCOL * NB)
```

```python
import functools

import jax
import jax.numpy as jnp
from jax import lax
from jax.experimental import pallas as pl
from jax.experimental.pallas import tpu as pltpu
from jax.sharding import PartitionSpec as P

NB = 256
CAP = 24
NZ, NX, NY = 16, 4, 4
NPROW = 2 * NZ
FAR = NZ // 2
SLOT = CAP * 4
TCH = 8
TROWS = 512 // TCH
GROUP = 4
BF, F32 = jnp.bfloat16, jnp.float32
VMEM, ANY, SMEM = pltpu.VMEM, pl.ANY, pltpu.SMEM


def spec(space):
    return pl.BlockSpec(memory_space=space)


def remote(src, dst, ss, rs, **where):
    return pltpu.make_async_remote_copy(
        src_ref=src, dst_ref=dst, send_sem=ss, recv_sem=rs,
        device_id=where, device_id_type=pl.DeviceIdType.MESH,
    )


def onehot(cond, value=1.0):
    return jnp.where(cond, value, 0.0).astype(BF)


def column_of(row):
    n = row.shape[1]
    eye = lax.broadcasted_iota(jnp.int32, (n, n), 0) == lax.broadcasted_iota(jnp.int32, (n, n), 1)
    return jnp.sum(jnp.where(eye, jnp.broadcast_to(row, (n, n)), 0), axis=1, keepdims=True)


def owner_of(piv):
    return (piv >> 8) & (NPROW - 1)


def ranks(row, col):
    i0 = lax.broadcasted_iota(jnp.int32, (NB, NB), 0)
    i1 = lax.broadcasted_iota(jnp.int32, (NB, NB), 1)
    before = (owner_of(col) == owner_of(row)) & (i1 < i0) & (row != i1)
    return jnp.dot(onehot(before), jnp.ones((NB, 128), BF), preferred_element_type=F32)


def pick_kernel(piv_ref, t_ref, row_ref, x_ref, o_ref, rounds_ref, idx_ref, sem):
    me = lax.axis_index("prow")
    first = t_ref[0] * CAP
    for s in range(CAP + 1):
        idx_ref[s] = 0

    def step(i, n):
        p = piv_ref[i]
        mine = (((p >> 8) & (NPROW - 1)) == me) & (p != i)
        at = n - first
        slot = jnp.where((at >= 0) & (at < CAP), at, CAP)
        idx_ref[slot] = ((p >> 13) << 8) + (p & 255)
        return n + jnp.where(mine, 1, 0)

    n = lax.fori_loop(0, NB, step, 0, unroll=8)

    @pl.when((n >= first) & (n < first + CAP))
    def _():
        idx_ref[n - first] = 0

    copies = []
    for s in range(CAP):
        r = idx_ref[s]
        copies.append(pltpu.make_async_copy(x_ref.at[r >> 8, r & 255], o_ref.at[s], sem.at[s]))
        copies[-1].start()
    row = row_ref[...]
    rank = ranks(row, column_of(row))
    rounds_ref[0] = jnp.max(rank).astype(jnp.int32) // CAP + 1
    for c in copies:
        c.wait()


def pick(trailing, pivots, t):
    out, rounds = pl.pallas_call(
        pick_kernel,
        out_shape=(
            jax.ShapeDtypeStruct((CAP, 2, 256), BF),
            jax.ShapeDtypeStruct((1,), jnp.int32),
        ),
        in_specs=[spec(SMEM), spec(SMEM), spec(VMEM), spec(ANY)],
        out_specs=(spec(VMEM), spec(SMEM)),
        scratch_shapes=[SMEM((CAP + 1,), jnp.int32), pltpu.SemaphoreType.DMA((CAP,))],
        compiler_params=pltpu.CompilerParams(vmem_limit_bytes=16 * 2**20),
        name="pick_rows",
    )(pivots, t, pivots.reshape(1, NB), trailing)
    return out.reshape(CAP, 2, 2, 128).transpose(0, 2, 1, 3).reshape(SLOT, 128), rounds


class Ring:
    def __init__(self, src, slots, zs, zr, ps, pr):
        self.src, self.slots, self.zs, self.zr, self.ps, self.pr = src, slots, zs, zr, ps, pr
        me = lax.axis_index("prow")
        self.z, self.core = me // 2, me % 2
        self.sent = []

    def rows(self, z, core):
        return self.slots.at[pl.ds(((z % NZ) * 2 + core) * SLOT, SLOT)]

    def hop(self, way, s, src=None):
        sign = 1 - 2 * way
        dst = self.rows(self.z + NZ - sign * s, self.core)
        to = ((self.z + NZ + sign) % NZ) * 2 + self.core
        c = remote(dst if src is None else src, dst, self.zs.at[way, s], self.zr.at[way, s], prow=to)
        c.start()
        self.sent.append(c)

    def mate(self, k, offset, src=None):
        dst = self.rows(self.z + NZ + offset, self.core)
        c = remote(
            dst if src is None else src, dst, self.ps.at[k], self.pr.at[k],
            prow=self.z * 2 + 1 - self.core,
        )
        c.start()
        self.sent.append(c)

    def begin(self):
        self.hop(0, 0, self.src)
        self.hop(1, 0, self.src)
        self.mate(0, 0, self.src)

    def arrive(self, way, s):
        sign = 1 - 2 * way
        dst = self.rows(self.z + NZ - sign * s, self.core)
        remote(
            dst, dst, self.zs.at[way, s - 1], self.zr.at[way, s - 1], prow=self.z * 2 + self.core
        ).wait_recv()

    def step(self, s):
        if s > FAR:
            return
        self.arrive(0, s)
        if s < FAR:
            self.hop(0, s)
        self.mate(s, -s)
        if s < FAR:
            self.arrive(1, s)
            if s < FAR - 1:
                self.hop(1, s)
            self.mate(FAR + s, s)

    def finish(self):
        for k in range(NZ):
            offset = -k if k <= FAR else k - FAR
            dst = self.rows(self.z + NZ + offset, 1 - self.core)
            remote(
                dst, dst, self.ps.at[k], self.pr.at[k], prow=self.z * 2 + self.core
            ).wait_recv()
        for c in self.sent:
            c.wait_send()


RING_SEMS = [
    pltpu.SemaphoreType.DMA((2, FAR)),
    pltpu.SemaphoreType.DMA((2, FAR)),
    pltpu.SemaphoreType.DMA((NZ,)),
    pltpu.SemaphoreType.DMA((NZ,)),
]


def greet(ids):
    barrier = pltpu.get_barrier_semaphore()
    for where in ids:
        pl.semaphore_signal(barrier, inc=1, device_id=where, device_id_type=pl.DeviceIdType.MESH)
    pl.semaphore_wait(barrier, len(ids))


def z_neighbours():
    me = lax.axis_index("prow")
    z, core = me // 2, me % 2
    return [
        {"prow": ((z + 1) % NZ) * 2 + core},
        {"prow": ((z + NZ - 1) % NZ) * 2 + core},
        {"prow": z * 2 + 1 - core},
    ]


def gather_kernel(src_ref, o_ref, slots, zs, zr, ps, pr, sem):
    greet(z_neighbours())
    ring = Ring(src_ref, slots, zs, zr, ps, pr)
    ring.begin()
    own = pltpu.make_async_copy(src_ref, ring.rows(ring.z, ring.core), sem)
    own.start()
    for s in range(1, FAR + 1):
        ring.step(s)
    own.wait()
    ring.finish()
    o_ref[...] = slots[...]


def gather_round(picked):
    return pl.pallas_call(
        gather_kernel,
        out_shape=jax.ShapeDtypeStruct((NPROW * SLOT, 128), BF),
        in_specs=[spec(VMEM)],
        out_specs=spec(VMEM),
        scratch_shapes=[VMEM((NPROW * SLOT, 128), BF)] + RING_SEMS + [pltpu.SemaphoreType.DMA],
        compiler_params=pltpu.CompilerParams(collective_id=1, has_side_effects=True),
        name="gather_more",
    )(picked)


def later_rounds(trailing, pivots, rounds):
    i = jnp.arange(NB, dtype=jnp.int32)
    owner = owner_of(pivots)
    moved = pivots != i
    before = (owner[:, None] == owner[None, :]) & (i[None, :] < i[:, None]) & moved[None, :]
    rank = jnp.sum(before.astype(jnp.int32), axis=1)

    def body(carry):
        t, total = carry
        picked, _ = pick(trailing, pivots, t.reshape(1))
        rows = gather_round(picked).reshape(NPROW * CAP, 512)
        at = rank - t * CAP
        slot = jnp.where(moved & (at >= 0) & (at < CAP), owner * CAP + at, -1)
        chosen = onehot(slot[:, None] == jnp.arange(NPROW * CAP, dtype=jnp.int32)[None, :])
        part = jnp.dot(chosen, rows, preferred_element_type=F32).astype(BF)
        return t + 1, total + part.reshape(NB * 4, 128)

    start = (jnp.int32(1), jnp.zeros((NB * 4, 128), BF))
    return lax.while_loop(lambda c: c[0] < rounds[0], body, start)[1]


class Plane:
    OFF = (0, -1, 1, 2)

    def __init__(self, src, out, ss, rs):
        self.src, self.out, self.ss, self.rs = src, out, ss, rs
        q = lax.axis_index("pcol")
        self.x, self.y = q // NY, q % NY
        self.sent = []

    def device(self, h, first, second):
        dx, dy = (second, first) if h == 0 else (first, second)
        return ((self.x + NX + dx) % NX) * NY + (self.y + NY + dy) % NY

    def part(self, h, first, second, quarter=None):
        base = self.device(h, first, second) * 256 + h * 128
        if quarter is None:
            return self.out.at[pl.ds(base, 128)]
        return self.out.at[pl.ds(base + 64 * quarter, 64)]

    def send(self, h, k, to, ref, src=None):
        c = remote(ref if src is None else src, ref, self.ss.at[h, k], self.rs.at[h, k], pcol=to)
        c.start()
        self.sent.append(c)

    def wait(self, h, k, ref):
        remote(ref, ref, self.ss.at[h, k], self.rs.at[h, k], pcol=self.device(h, 0, 0)).wait_recv()

    def second(self, h, m, src=None):
        ref = self.part(h, self.OFF[m], 0)
        self.send(h, 4 + m, self.device(h, 0, 1), ref, src)
        self.send(h, 8 + m, self.device(h, 0, -1), ref, src)

    def begin(self):
        for h in range(2):
            own = self.src.at[pl.ds(h * 128, 128)]
            self.send(h, 0, self.device(h, 1, 0), self.part(h, 0, 0), own)
            self.send(h, 1, self.device(h, -1, 0), self.part(h, 0, 0), own)
        for h in range(2):
            self.second(h, 0, self.src.at[pl.ds(h * 128, 128)])

    def one(self):
        for h in range(2):
            self.wait(h, 0, self.part(h, -1, 0))
            self.send(h, 2, self.device(h, 1, 0), self.part(h, -1, 0, 0))
            self.wait(h, 1, self.part(h, 1, 0))
            self.send(h, 3, self.device(h, -1, 0), self.part(h, 1, 0, 1))
        for h in range(2):
            self.second(h, 1)
            self.second(h, 2)

    def two(self):
        for h in range(2):
            self.wait(h, 2, self.part(h, -2, 0, 0))
            self.wait(h, 3, self.part(h, 2, 0, 1))
            self.second(h, 3)

    def three(self, m):
        for h in range(2):
            f = self.OFF[m]
            self.wait(h, 4 + m, self.part(h, f, -1))
            self.send(h, 12 + m, self.device(h, 0, 1), self.part(h, f, -1, 0))
            self.wait(h, 8 + m, self.part(h, f, 1))
            self.send(h, 16 + m, self.device(h, 0, -1), self.part(h, f, 1, 1))

    def four(self):
        for h in range(2):
            for m in range(4):
                self.wait(h, 12 + m, self.part(h, self.OFF[m], -2, 0))
                self.wait(h, 16 + m, self.part(h, self.OFF[m], 2, 1))

    def finish(self):
        for c in self.sent:
            c.wait_send()


def plane_neighbours():
    q = lax.axis_index("pcol")
    x, y = q // NY, q % NY
    return [
        {"pcol": ((x + 1) % NX) * NY + y},
        {"pcol": ((x + NX - 1) % NX) * NY + y},
        {"pcol": x * NY + (y + 1) % NY},
        {"pcol": x * NY + (y + NY - 1) % NY},
    ]


class Top:
    def __init__(self, src, out, ss, rr, ps, pr):
        self.src, self.out, self.ss, self.rr, self.ps, self.pr = src, out, ss, rr, ps, pr
        me = lax.axis_index("prow")
        self.z, self.core = me // 2, me % 2
        self.dist = jnp.where(self.z <= FAR, self.z, NZ - self.z)
        self.root = me == 0
        self.right = self.z < FAR
        self.left = (self.z == 0) | (self.z > FAR + 1)

    def rows(self, ref, half, n):
        return ref.at[pl.ds(half * 512 + n * TROWS, TROWS)]

    def ring(self, way, n, src):
        to = ((self.z + NZ + 1 - 2 * way) % NZ) * 2 + self.core
        return remote(
            self.rows(src, self.core, n), self.rows(self.out, self.core, n),
            self.ss.at[way, n], self.rr.at[n], prow=to,
        )

    def mate(self, half, n, src, rsem):
        return remote(
            self.rows(src, half, n), self.rows(self.out, half, n),
            self.ps.at[half, n], rsem.at[n], prow=self.z * 2 + 1 - self.core,
        )

    def begin(self):
        @pl.when(self.root)
        def _():
            for n in range(TCH):
                self.mate(1, n, self.src, self.rr).start()
                self.ring(0, n, self.src).start()
                self.ring(1, n, self.src).start()
            for n in range(TCH):
                self.mate(0, n, self.src, self.pr).start()

    def own(self, sem):
        return pltpu.make_async_copy(self.src.at[pl.ds(0, 1024)], self.out, sem)

    def step(self, s):
        for g in range(TCH // GROUP):
            @pl.when((self.dist + g == s) & ~self.root)
            def _():
                for n in range(g * GROUP, (g + 1) * GROUP):
                    self.ring(0, n, self.out).wait_recv()

                    @pl.when(self.right)
                    def _():
                        self.ring(0, n, self.out).start()

                    @pl.when(self.left)
                    def _():
                        self.ring(1, n, self.out).start()

                    @pl.when(self.z != 0)
                    def _():
                        self.mate(self.core, n, self.out, self.pr).start()

    def finish(self):
        @pl.when(~self.root)
        def _():
            for n in range(TCH):
                self.mate(1 - self.core, n, self.out, self.pr).wait_recv()

        @pl.when(self.right)
        def _():
            for n in range(TCH):
                self.ring(0, n, self.out).wait_send()

        @pl.when(self.left)
        def _():
            for n in range(TCH):
                self.ring(1, n, self.out).wait_send()

        @pl.when(self.z != 0)
        def _():
            for n in range(TCH):
                self.mate(self.core, n, self.out, self.pr).wait_send()

        @pl.when(self.root)
        def _():
            for n in range(TCH):
                self.mate(0, n, self.src, self.pr).wait_send()
                self.mate(1, n, self.src, self.rr).wait_send()


TOP_SEMS = [
    pltpu.SemaphoreType.DMA((2, TCH)),
    pltpu.SemaphoreType.DMA((TCH,)),
    pltpu.SemaphoreType.DMA((2, TCH)),
    pltpu.SemaphoreType.DMA((TCH,)),
]


def main_kernel(
    x_ref, pick_ref, panel_ref, linv_ref, uinv_ref, row_ref, extra_ref,
    m_ref, xm_ref, st_ref,
    slots, top, panel, panelf, wide, both, mask,
    zs, zr, zps, zpr, ts, tr, tps, tpr, ss, rs, sems,
):
    me = lax.axis_index("prow")
    fetch = pltpu.make_async_copy(x_ref, xm_ref, sems.at[0])
    fetch.start()
    greet(z_neighbours() + plane_neighbours())
    ring = Ring(pick_ref, slots, zs, zr, zps, zpr)
    plane = Plane(panel_ref, panel, ss, rs)
    head = Top(x_ref, top, ts, tr, tps, tpr)
    head.begin()
    ring.begin()
    plane.begin()
    q = lax.axis_index("pcol")
    own_panel = pltpu.make_async_copy(panel_ref, panel.at[pl.ds(q * 256, 256)], sems.at[1])
    own_panel.start()
    own_slot = pltpu.make_async_copy(pick_ref, ring.rows(ring.z, ring.core), sems.at[2])
    own_slot.start()

    @pl.when(head.root)
    def _():
        head.own(sems.at[3]).start()

    row = row_ref[...]
    lanes = lax.broadcasted_iota(jnp.int32, (1, NB), 1)
    moved = row != lanes

    def swaps(b):
        rows = lax.broadcasted_iota(jnp.int32, (NB, NB), 0) + (b * NPROW + me) * NB
        hit = (rows == row) & moved
        m_ref[pl.ds(b * NB, NB), NB:] = onehot(hit, -1.0)
        gone = jnp.dot(onehot(hit), jnp.ones((NB, 128), BF), preferred_element_type=F32)
        for j in range(4):
            mask[pl.ds(j, NB, stride=4), :] = gone
        x = xm_ref[pl.ds(b * 1024, 1024), :].astype(F32)
        xm_ref[pl.ds(b * 1024, 1024), :] = jnp.where(mask[...] > 0.5, 0.0, x).astype(BF)

    def lower(k):
        piece = panelf[pl.ds((k % 2) * 8 + k // 2, NB, stride=16), :].astype(BF)
        low = lax.dot_general(
            piece, uinv_ref[...], (((0,), (0,)), ((), ())), preferred_element_type=F32
        )
        m_ref[pl.ds(k * 128, 128), :NB] = low.astype(BF)

    head.step(0)
    fetch.wait()
    for s in range(1, FAR + 3):
        ring.step(s)
        head.step(s)
        if s == 1:
            plane.one()
        if s == 2:
            plane.two()
        if 3 <= s <= 6:
            plane.three(s - 3)
        if s == 7:
            plane.four()
            own_panel.wait()
        if s <= 4:
            swaps(2 * s - 2)
            swaps(2 * s - 1)
        if s == 7:
            panelf[...] = panel[...].astype(F32)
        if s in (8, 9):
            for k in range(8 * (s - 8), 8 * (s - 7)):
                lower(k)
    col = column_of(row)
    rank = ranks(row, col).astype(jnp.int32)
    ids = lax.broadcasted_iota(jnp.int32, (NB, 128), 0)
    lane = lax.broadcasted_iota(jnp.int32, (NB, 128), 1)
    goes = jnp.broadcast_to(col, (NB, 128)) != ids
    slot = jnp.where(
        goes & (rank < CAP), owner_of(jnp.broadcast_to(col, (NB, 128))) * CAP + rank, -1
    )
    stay = jnp.where(goes, -1, ids + NPROW * CAP)
    pieces = [onehot((slot == lane + 128 * u) | (stay == lane + 128 * u)) for u in range(8)]
    chosen = jnp.concatenate(pieces, axis=1)

    own_slot.wait()

    @pl.when(head.root)
    def _():
        head.own(sems.at[3]).wait()

    ring.finish()
    head.finish()
    plane.finish()
    wide[pl.ds(0, NPROW * SLOT), :] = slots[...].astype(F32)
    wide[pl.ds(NPROW * SLOT, 1024), :] = top[...].astype(F32)
    for j in range(4):
        both[:, j * 128 : (j + 1) * 128] = wide[pl.ds(j, 1024, stride=4), :].astype(BF)
    picked = jnp.dot(chosen, both[...], preferred_element_type=F32)
    wide[pl.ds(0, 1024), :] = extra_ref[...].astype(F32)
    more = jnp.concatenate([wide[pl.ds(j, NB, stride=4), :] for j in range(4)], axis=1)
    picked = (picked + more).astype(BF)
    st_ref[pl.ds(0, NB), :] = jnp.dot(
        linv_ref[...], picked, preferred_element_type=F32
    ).astype(BF)
    st_ref[pl.ds(NB, NB), :] = both[pl.ds(NPROW * CAP, NB), :]


def main(tv, picked, pv, linv, uinv, row, extra):
    return pl.pallas_call(
        main_kernel,
        out_shape=(
            jax.ShapeDtypeStruct((8 * NB, 2 * NB), BF),
            jax.ShapeDtypeStruct((8192, 128), BF),
            jax.ShapeDtypeStruct((2 * NB, 2 * NB), BF),
        ),
        in_specs=[spec(ANY)] + [spec(VMEM)] * 6,
        out_specs=(spec(VMEM),) * 3,
        scratch_shapes=[
            VMEM((NPROW * SLOT, 128), BF),
            VMEM((1024, 128), BF),
            VMEM((4096, 128), BF),
            VMEM((4096, 128), F32),
            VMEM((4096, 128), F32),
            VMEM((1024, 512), BF),
            VMEM((1024, 128), F32),
        ]
        + RING_SEMS
        + TOP_SEMS
        + [pltpu.SemaphoreType.DMA((2, 20)), pltpu.SemaphoreType.DMA((2, 20))]
        + [pltpu.SemaphoreType.DMA((4,))],
        compiler_params=pltpu.CompilerParams(
            collective_id=0, has_side_effects=True, vmem_limit_bytes=40 * 2**20
        ),
        name="gather_prepare",
    )(tv, picked, pv, linv, uinv, row, extra)


def update_kernel(m_ref, xm_ref, st_ref, o_ref, spread):
    i = pl.program_id(0)
    product = jnp.dot(
        m_ref[pl.ds(pl.multiple_of(i * NB, NB), NB), :], st_ref[...], preferred_element_type=F32
    )
    for j in range(4):
        spread[pl.ds(j, NB, stride=4), :] = product[:, j * 128 : (j + 1) * 128]
    x = xm_ref[pl.ds(pl.multiple_of(i * 1024, 1024), 1024), :]
    o_ref[...] = (x.astype(F32) - spread[...]).astype(BF)

    @pl.when((i == 0) & (lax.axis_index("prow") == 0))
    def _():
        for j in range(4):
            spread[pl.ds(j, NB, stride=4), :] = st_ref[pl.ds(0, NB), j * 128 : (j + 1) * 128].astype(F32)
        o_ref[...] = spread[...].astype(BF)


def update(m, xm, st):
    return pl.pallas_call(
        update_kernel,
        out_shape=jax.ShapeDtypeStruct((8192, 128), BF),
        grid=(8,),
        in_specs=[spec(VMEM)] * 3,
        out_specs=pl.BlockSpec((1024, 128), lambda i: (i, 0)),
        scratch_shapes=[VMEM((1024, 128), F32)],
        compiler_params=pltpu.CompilerParams(vmem_limit_bytes=16 * 2**20),
        name="update",
    )(m, xm, st)


def per_device(trailing, panel, lower_inverse, upper_inverse, pivots):
    tv = trailing.reshape(8, 256, 2, 2, 128).transpose(0, 1, 3, 2, 4).reshape(8192, 128)
    pv = panel.reshape(16, 8, 2, 128).transpose(0, 2, 1, 3).reshape(256, 128)
    picked, rounds = pick(trailing, pivots, jnp.zeros((1,), jnp.int32))
    extra = later_rounds(trailing, pivots, rounds)
    m, xm, st = main(
        tv, picked, pv, lower_inverse, upper_inverse, pivots.reshape(1, NB), extra
    )
    out = update(m, xm, st)
    return out.reshape(8, 256, 2, 2, 128).transpose(0, 1, 3, 2, 4).reshape(trailing.shape)


def solution(mesh):
    placed = (P(None, "prow", None, "pcol"), P("pcol", None, "prow"), P(), P(), P())
    return jax.shard_map(
        per_device,
        mesh=mesh,
        in_specs=placed,
        out_specs=P(None, "prow", None, "pcol"),
        check_vma=False,
    )
```

```python
import functools

import jax
import jax.numpy as jnp
from jax import lax
from jax.experimental import pallas as pl
from jax.experimental.pallas import tpu as pltpu
from jax.sharding import PartitionSpec as P

NB = 256
CAP = 20
NZ, NX, NY = 16, 4, 4
NPROW = 2 * NZ
KR = 2
LEVEL = (0, 4, 6, 16)
FAR = NZ // 2
WIDE = NPROW * CAP + NB
SLOT = CAP * 4
TCH = 4
TROWS = 512 // TCH
BF, F32 = jnp.bfloat16, jnp.float32
VMEM, ANY, SMEM = pltpu.VMEM, pl.ANY, pltpu.SMEM


def spec(space):
    return pl.BlockSpec(memory_space=space)


def remote(src, dst, ss, rs, **where):
    return pltpu.make_async_remote_copy(
        src_ref=src, dst_ref=dst, send_sem=ss, recv_sem=rs,
        device_id=where, device_id_type=pl.DeviceIdType.MESH,
    )


def onehot(cond, value=1.0):
    return jnp.where(cond, value, 0.0).astype(BF)


def column_of(row):
    n = row.shape[1]
    eye = lax.broadcasted_iota(jnp.int32, (n, n), 0) == lax.broadcasted_iota(jnp.int32, (n, n), 1)
    return jnp.sum(jnp.where(eye, jnp.broadcast_to(row, (n, n)), 0), axis=1, keepdims=True)


def owner_of(piv):
    return (piv >> 8) & (NPROW - 1)


def ranks(row, col):
    i0 = lax.broadcasted_iota(jnp.int32, (NB, NB), 0)
    i1 = lax.broadcasted_iota(jnp.int32, (NB, NB), 1)
    before = (owner_of(col) == owner_of(row)) & (i1 < i0) & (row != i1)
    return jnp.dot(onehot(before), jnp.ones((NB, 128), BF), preferred_element_type=F32)


def pick_kernel(t_ref, row_ref, x_ref, o_ref, rounds_ref, sem):
    me = lax.axis_index("prow")
    row = row_ref[...]
    col = column_of(row)
    rank = ranks(row, col).astype(jnp.int32)
    ids = lax.broadcasted_iota(jnp.int32, (NB, 128), 0)
    lane = lax.broadcasted_iota(jnp.int32, (NB, 128), 1)
    col = jnp.broadcast_to(col, (NB, 128))
    moved = col != ids
    here = moved & (owner_of(col) == me) & (rank == lane + t_ref[0] * CAP)
    local = ((col >> 13) << 8) + (col & 255)
    index = jnp.sum(jnp.where(here, local, 0), axis=0, keepdims=True)
    copies = []
    for s in range(CAP):
        r = jnp.sum(jnp.where(lane[:1] == s, index, 0))
        copies.append(pltpu.make_async_copy(x_ref.at[r >> 8, r & 255], o_ref.at[s], sem.at[s]))
        copies[-1].start()
    rounds_ref[0] = jnp.max(jnp.where(moved, rank, 0)) // CAP + 1
    for c in copies:
        c.wait()


def pick(trailing, row, t):
    out, rounds = pl.pallas_call(
        pick_kernel,
        out_shape=(
            jax.ShapeDtypeStruct((CAP, 2, 256), BF),
            jax.ShapeDtypeStruct((1,), jnp.int32),
        ),
        in_specs=[spec(SMEM), spec(VMEM), spec(ANY)],
        out_specs=(spec(VMEM), spec(SMEM)),
        scratch_shapes=[pltpu.SemaphoreType.DMA((CAP,))],
        compiler_params=pltpu.CompilerParams(vmem_limit_bytes=16 * 2**20),
        name="pick_rows",
    )(t, row, trailing)
    return out.reshape(CAP, 2, 2, 128).transpose(0, 2, 1, 3).reshape(SLOT, 128), rounds


class Ring:
    def __init__(self, src, slots, zs, zr, ps, pr):
        self.src, self.slots, self.zs, self.zr, self.ps, self.pr = src, slots, zs, zr, ps, pr
        me = lax.axis_index("prow")
        self.z, self.core = me // 2, me % 2

    def rows(self, z, core):
        return self.slots.at[pl.ds(((z % NZ) * 2 + core) * SLOT, SLOT)]

    def to(self, way, hops):
        return ((self.z + NZ + (1 - 2 * way) * hops) % NZ) * 2 + self.core

    def send(self, way, o, hops, src=None):
        dst = self.rows(self.z + NZ - (1 - 2 * way) * (o - hops), self.core)
        c = remote(
            dst if src is None else src, dst, self.zs, self.zr.at[way, o - 1],
            prow=self.to(way, hops),
        )
        c.start()

    def mate(self, offset, src=None):
        dst = self.rows(self.z + NZ + offset, self.core)
        c = remote(
            dst if src is None else src, dst, self.ps, self.pr, prow=self.z * 2 + 1 - self.core
        )
        c.start()

    def begin(self):
        for o in range(KR, 0, -1):
            for way in range(2):
                self.send(way, o, o, self.src)
        self.mate(0, self.src)

    def step(self, o):
        for way in range(2):
            last = FAR - way
            if o > last:
                continue
            dst = self.rows(self.z + NZ - (1 - 2 * way) * o, self.core)
            remote(
                dst, dst, self.zs, self.zr.at[way, o - 1], prow=self.to(0, 0)
            ).wait_recv()
            if o + KR <= last:
                self.send(way, o + KR, KR)
            self.mate(o * (2 * way - 1))

    def finish(self):
        mates = self.slots.at[pl.ds(0, NZ * SLOT)]
        mate = remote(mates, mates, self.ps, self.pr, prow=self.to(0, 0))
        mate.wait_recv()
        mate.wait_send()
        sent = self.slots.at[pl.ds(0, (NZ - 1) * SLOT)]
        remote(sent, sent, self.zs, self.pr, prow=self.to(0, 0)).wait_send()


DMA = pltpu.SemaphoreType.DMA
RING_SEMS = [DMA, DMA((2, FAR)), DMA, DMA]


def greet(ids, meanwhile=None):
    barrier = pltpu.get_barrier_semaphore()
    for where in ids:
        pl.semaphore_signal(barrier, inc=1, device_id=where, device_id_type=pl.DeviceIdType.MESH)
    if meanwhile is not None:
        meanwhile()
    pl.semaphore_wait(barrier, len(ids))


def z_neighbours():
    me = lax.axis_index("prow")
    z, core = me // 2, me % 2
    away = [d for k in range(1, max(KR, 2) + 1) for d in (k, NZ - k)]
    return [{"prow": z * 2 + 1 - core}] + [{"prow": ((z + d) % NZ) * 2 + core} for d in away]


def gather_kernel(src_ref, o_ref, slots, zs, zr, ps, pr, sem):
    greet(z_neighbours())
    ring = Ring(src_ref, slots, zs, zr, ps, pr)
    ring.begin()
    own = pltpu.make_async_copy(src_ref, ring.rows(ring.z, ring.core), sem)
    own.start()
    for s in range(1, FAR + 1):
        ring.step(s)
    own.wait()
    ring.finish()
    o_ref[...] = slots[...]


def gather_round(picked):
    return pl.pallas_call(
        gather_kernel,
        out_shape=jax.ShapeDtypeStruct((NPROW * SLOT, 128), BF),
        in_specs=[spec(VMEM)],
        out_specs=spec(VMEM),
        scratch_shapes=[VMEM((NPROW * SLOT, 128), BF)] + RING_SEMS + [pltpu.SemaphoreType.DMA],
        compiler_params=pltpu.CompilerParams(collective_id=1, has_side_effects=True),
        name="gather_more",
    )(picked)


def later_rounds(trailing, row, rounds):
    def body(carry):
        t, total = carry
        picked, _ = pick(trailing, row, t.reshape(1))
        rows = gather_round(picked).reshape(NPROW * CAP, 512)
        pivots = row[0] + jnp.minimum(t, 0)
        i = jnp.arange(NB, dtype=jnp.int32)
        owner = owner_of(pivots)
        moved = pivots != i
        before = (owner[:, None] == owner[None, :]) & (i[None, :] < i[:, None]) & moved[None, :]
        at = jnp.sum(before.astype(jnp.int32), axis=1) - t * CAP
        slot = jnp.where(moved & (at >= 0) & (at < CAP), owner * CAP + at, -1)
        chosen = onehot(slot[:, None] == jnp.arange(NPROW * CAP, dtype=jnp.int32)[None, :])
        part = jnp.dot(chosen, rows, preferred_element_type=F32).astype(BF)
        return t + 1, total + part.reshape(NB * 4, 128)

    start = (jnp.int32(1), jnp.zeros((NB * 4, 128), BF))
    return lax.while_loop(lambda c: c[0] < rounds[0], body, start)[1]


class Plane:
    OFF = (0, -1, 1, 2)

    def __init__(self, src, out, ss, rs, last):
        self.src, self.out, self.ss, self.rs, self.last = src, out, ss, rs, last
        q = lax.axis_index("pcol")
        self.x, self.y = q // NY, q % NY

    def device(self, h, first, second):
        dx, dy = (second, first) if h == 0 else (first, second)
        return ((self.x + NX + dx) % NX) * NY + (self.y + NY + dy) % NY

    def part(self, h, first, second, quarter=None):
        base = self.device(h, first, second) * 256 + h * 128
        if quarter is None:
            return self.out.at[pl.ds(base, 128)]
        return self.out.at[pl.ds(base + 64 * quarter, 64)]

    def send(self, h, k, to, ref, src=None):
        rs = self.last if k >= 12 else self.rs.at[h, k]
        remote(ref if src is None else src, ref, self.ss, rs, pcol=to).start()

    def wait(self, h, k, ref):
        remote(ref, ref, self.ss, self.rs.at[h, k], pcol=self.device(h, 0, 0)).wait_recv()

    def second(self, h, m, src=None):
        ref = self.part(h, self.OFF[m], 0)
        self.send(h, 4 + m, self.device(h, 0, 1), ref, src)
        self.send(h, 8 + m, self.device(h, 0, -1), ref, src)

    def begin(self):
        for h in range(2):
            own = self.src.at[pl.ds(h * 128, 128)]
            for k, f in enumerate((2, 1, -1)):
                self.send(h, k, self.device(h, f, 0), self.part(h, 0, 0), own)
        for h in range(2):
            self.second(h, 0, self.src.at[pl.ds(h * 128, 128)])

    def one(self):
        for h in range(2):
            self.wait(h, 1, self.part(h, -1, 0))
            self.second(h, 1)
        for h in range(2):
            self.wait(h, 2, self.part(h, 1, 0))
            self.second(h, 2)

    def two(self):
        for h in range(2):
            self.wait(h, 0, self.part(h, -2, 0))
            self.second(h, 3)

    def three(self, m):
        for h in range(2):
            f = self.OFF[m]
            self.wait(h, 4 + m, self.part(h, f, -1))
            self.send(h, 12 + m, self.device(h, 0, 1), self.part(h, f, -1, 0))
            self.wait(h, 8 + m, self.part(h, f, 1))
            self.send(h, 16 + m, self.device(h, 0, -1), self.part(h, f, 1, 1))

    def four(self):
        got = self.out.at[pl.ds(0, 1024)]
        remote(got, got, self.ss, self.last, pcol=self.device(0, 0, 0)).wait_recv()

    def finish(self):
        sent = self.out.at[pl.ds(0, 3840)]
        remote(sent, sent, self.ss, self.last, pcol=self.device(0, 0, 0)).wait_send()


def plane_neighbours():
    q = lax.axis_index("pcol")
    x, y = q // NY, q % NY
    along_x = [{"pcol": ((x + d) % NX) * NY + y} for d in range(1, NX)]
    return along_x + [{"pcol": x * NY + (y + d) % NY} for d in range(1, NY)]


class Top:
    KINDS = ((0, 2), (1, 2), (0, 1), (1, 1))

    def __init__(self, src, out, ss, rr, ps, pr):
        self.src, self.out, self.ss, self.rr, self.ps, self.pr = src, out, ss, rr, ps, pr
        me = lax.axis_index("prow")
        z = me // 2
        self.z, self.core = z, me % 2
        self.root = me == 0
        self.dist = jnp.where(z <= FAR, z, NZ - z)
        self.relay = z % 2 == 0
        self.goes = (
            self.relay & (z <= FAR - 2),
            self.relay & ((z == 0) | (z >= FAR + 4)),
            self.relay & (z >= FAR + 2),
            self.relay & (((z >= 2) & (z <= FAR)) | (z == FAR + 2)),
        )

    def rows(self, ref, half, n):
        return ref.at[pl.ds(half * 512 + n * TROWS, TROWS)]

    def half(self, half):
        return self.out.at[pl.ds(half * 512, 512)]

    def ring(self, k, n, src):
        way, hops = self.KINDS[k]
        to = ((self.z + NZ + (1 - 2 * way) * hops) % NZ) * 2 + self.core
        return remote(
            self.rows(src, self.core, n), self.rows(self.out, self.core, n),
            self.ss.at[k], self.rr.at[n], prow=to,
        )

    def mate(self, half, n, src, rsem):
        return remote(
            self.rows(src, half, n), self.rows(self.out, half, n),
            self.ps.at[half], rsem, prow=self.z * 2 + 1 - self.core,
        )

    def begin(self):
        @pl.when(self.root)
        def _():
            for n in range(TCH):
                self.mate(1, n, self.src, self.rr.at[n]).start()
                self.ring(0, n, self.src).start()
                self.ring(1, n, self.src).start()
            for n in range(TCH):
                self.mate(0, n, self.src, self.pr).start()

    def own(self, sem):
        return pltpu.make_async_copy(self.src.at[pl.ds(0, 1024)], self.out, sem)

    def step(self, who, chunks):
        @pl.when(who & ~self.root)
        def _():
            for n in chunks:
                self.ring(0, n, self.out).wait_recv()
                for k in range(4):
                    @pl.when(self.goes[k])
                    def _():
                        self.ring(k, n, self.out).start()

                @pl.when(self.z != 0)
                def _():
                    self.mate(self.core, n, self.out, self.pr).start()

    def finish(self):
        other, own = self.half(1 - self.core), self.half(self.core)
        me = self.z * 2 + self.core

        @pl.when(~self.root)
        def _():
            remote(other, other, self.ss.at[0], self.pr, prow=me).wait_recv()

        for k in range(4):
            @pl.when(self.goes[k])
            def _():
                remote(own, own, self.ss.at[k], self.pr, prow=me).wait_send()

        @pl.when(self.z != 0)
        def _():
            remote(own, own, self.ps.at[self.core], self.pr, prow=me).wait_send()

        @pl.when(self.root)
        def _():
            for half in range(2):
                ref = self.half(half)
                remote(ref, ref, self.ps.at[half], self.pr, prow=me).wait_send()


TOP_SEMS = [DMA((4,)), DMA((TCH,)), DMA((2,)), DMA]


def main_kernel(
    x_ref, pick_ref, panel_ref, linv_ref, uinv_ref, row_ref, extra_ref,
    m_ref, xm_ref, st_ref,
    slots, top, panel, panelf, wide, both, mask,
    zs, zr, zps, zpr, ts, tr, tps, tpr, ss, rs, last, sems,
):
    me = lax.axis_index("prow")
    ring = Ring(pick_ref, slots, zs, zr, zps, zpr)
    plane = Plane(panel_ref, panel, ss, rs, last)
    head = Top(x_ref, top, ts, tr, tps, tpr)
    row = row_ref[...]
    lanes = lax.broadcasted_iota(jnp.int32, (1, NB), 1)
    moved = row != lanes

    def swaps(b):
        rows = lax.broadcasted_iota(jnp.int32, (NB, NB), 0) + (b * NPROW + me) * NB
        hit = (rows == row) & moved
        m_ref[pl.ds(b * NB, NB), NB:] = onehot(hit, -1.0)
        gone = jnp.dot(onehot(hit), jnp.ones((NB, 128), BF), preferred_element_type=F32)
        for j in range(4):
            mask[pl.ds(j, NB, stride=4), :] = gone
        x = x_ref[pl.ds(b * 1024, 1024), :].astype(F32)
        xm_ref[pl.ds(b * 1024, 1024), :] = jnp.where(mask[...] > 0.5, 0.0, x).astype(BF)

    def lower(k):
        piece = panelf[pl.ds((k % 2) * 8 + k // 2, NB, stride=16), :].astype(BF)
        low = lax.dot_general(
            piece, uinv_ref[...], (((0,), (0,)), ((), ())), preferred_element_type=F32
        )
        m_ref[pl.ds(k * 128, 128), :NB] = low.astype(BF)

    def masks():
        for b in range(8):
            swaps(b)

    greet(z_neighbours() + plane_neighbours(), masks)
    head.begin()
    ring.begin()
    plane.begin()
    q = lax.axis_index("pcol")
    own_panel = pltpu.make_async_copy(panel_ref, panel.at[pl.ds(q * 256, 256)], sems.at[0])
    own_panel.start()
    own_slot = pltpu.make_async_copy(pick_ref, ring.rows(ring.z, ring.core), sems.at[1])
    own_slot.start()

    @pl.when(head.root)
    def _():
        head.own(sems.at[2]).start()

    near, middle, far = [head.relay & ((head.dist >= LEVEL[k]) & (head.dist < LEVEL[k + 1])) for k in range(3)]
    first, second = range(TCH // 2), range(TCH // 2, TCH)
    ring.step(1)
    ring.step(2)
    plane.one()
    plane.two()
    plane.three(0)
    head.step(near, first)
    ring.step(3)
    ring.step(4)
    head.step(near, second)
    head.step(middle, first)
    plane.three(1)
    plane.three(2)
    ring.step(5)
    ring.step(6)
    head.step(middle, second)
    plane.three(3)
    head.step(far, first)
    ring.step(7)
    ring.step(8)
    head.step(far, second)
    plane.four()
    own_panel.wait()
    panelf[...] = panel[...].astype(F32)
    for k in range(16):
        lower(k)
    head.step(~head.relay, range(TCH))
    col = column_of(row)
    rank = ranks(row, col).astype(jnp.int32)
    ids = lax.broadcasted_iota(jnp.int32, (NB, 128), 0)
    lane = lax.broadcasted_iota(jnp.int32, (NB, 128), 1)
    goes = jnp.broadcast_to(col, (NB, 128)) != ids
    slot = jnp.where(
        goes & (rank < CAP), owner_of(jnp.broadcast_to(col, (NB, 128))) * CAP + rank, -1
    )
    stay = jnp.where(goes, -1, ids + NPROW * CAP)
    pieces = [onehot((slot == lane + 128 * u) | (stay == lane + 128 * u)) for u in range(WIDE // 128)]
    chosen = jnp.concatenate(pieces, axis=1)

    own_slot.wait()

    @pl.when(head.root)
    def _():
        head.own(sems.at[2]).wait()

    ring.finish()
    head.finish()
    plane.finish()
    wide[pl.ds(0, NPROW * SLOT), :] = slots[...].astype(F32)
    wide[pl.ds(NPROW * SLOT, 1024), :] = top[...].astype(F32)
    for j in range(4):
        both[:, j * 128 : (j + 1) * 128] = wide[pl.ds(j, WIDE, stride=4), :].astype(BF)
    picked = jnp.dot(chosen, both[...], preferred_element_type=F32)
    wide[pl.ds(0, 1024), :] = extra_ref[...].astype(F32)
    more = jnp.concatenate([wide[pl.ds(j, NB, stride=4), :] for j in range(4)], axis=1)
    picked = (picked + more).astype(BF)
    st_ref[pl.ds(0, NB), :] = jnp.dot(
        linv_ref[...], picked, preferred_element_type=F32
    ).astype(BF)
    st_ref[pl.ds(NB, NB), :] = both[pl.ds(NPROW * CAP, NB), :]


def main(tv, picked, pv, linv, uinv, row, extra):
    return pl.pallas_call(
        main_kernel,
        out_shape=(
            jax.ShapeDtypeStruct((8 * NB, 2 * NB), BF),
            jax.ShapeDtypeStruct((8192, 128), BF),
            jax.ShapeDtypeStruct((2 * NB, 2 * NB), BF),
        ),
        in_specs=[spec(VMEM)] * 7,
        out_specs=(spec(VMEM),) * 3,
        scratch_shapes=[
            VMEM((NPROW * SLOT, 128), BF),
            VMEM((1024, 128), BF),
            VMEM((4096, 128), BF),
            VMEM((4096, 128), F32),
            VMEM((4 * WIDE, 128), F32),
            VMEM((WIDE, 512), BF),
            VMEM((1024, 128), F32),
        ]
        + RING_SEMS
        + TOP_SEMS
        + [DMA, DMA((2, 12)), DMA]
        + [DMA((3,))],
        compiler_params=pltpu.CompilerParams(
            collective_id=0, has_side_effects=True, vmem_limit_bytes=40 * 2**20
        ),
        name="gather_prepare",
    )(tv, picked, pv, linv, uinv, row, extra)


def update_kernel(m_ref, xm_ref, st_ref, o_ref, spread):
    i = pl.program_id(0)
    product = jnp.dot(
        m_ref[pl.ds(pl.multiple_of(i * NB, NB), NB), :], st_ref[...], preferred_element_type=F32
    )
    for j in range(4):
        spread[pl.ds(j, NB, stride=4), :] = product[:, j * 128 : (j + 1) * 128]
    x = xm_ref[pl.ds(pl.multiple_of(i * 1024, 1024), 1024), :]
    o_ref[...] = (x.astype(F32) - spread[...]).astype(BF)

    @pl.when((i == 0) & (lax.axis_index("prow") == 0))
    def _():
        for j in range(4):
            spread[pl.ds(j, NB, stride=4), :] = st_ref[pl.ds(0, NB), j * 128 : (j + 1) * 128].astype(F32)
        o_ref[...] = spread[...].astype(BF)


def update(m, xm, st):
    return pl.pallas_call(
        update_kernel,
        out_shape=jax.ShapeDtypeStruct((8192, 128), BF),
        grid=(8,),
        in_specs=[spec(VMEM)] * 3,
        out_specs=pl.BlockSpec((1024, 128), lambda i: (i, 0)),
        scratch_shapes=[VMEM((1024, 128), F32)],
        compiler_params=pltpu.CompilerParams(vmem_limit_bytes=16 * 2**20),
        name="update",
    )(m, xm, st)


def per_device(trailing, panel, lower_inverse, upper_inverse, pivots):
    tv = trailing.reshape(8, 256, 2, 2, 128).transpose(0, 1, 3, 2, 4).reshape(8192, 128)
    pv = panel.reshape(16, 8, 2, 128).transpose(0, 2, 1, 3).reshape(256, 128)
    row = pivots.reshape(1, NB)
    picked, rounds = pick(trailing, row, jnp.zeros((1,), jnp.int32))
    extra = later_rounds(trailing, row, rounds)
    m, xm, st = main(tv, picked, pv, lower_inverse, upper_inverse, row, extra)
    out = update(m, xm, st)
    return out.reshape(8, 256, 2, 2, 128).transpose(0, 1, 3, 2, 4).reshape(trailing.shape)


def solution(mesh):
    placed = (P(None, "prow", None, "pcol"), P("pcol", None, "prow"), P(), P(), P())
    return jax.shard_map(
        per_device,
        mesh=mesh,
        in_specs=placed,
        out_specs=P(None, "prow", None, "pcol"),
        check_vma=False,
    )
```

```python
import functools

import jax
import jax.numpy as jnp
from jax import lax
from jax.experimental import pallas as pl
from jax.experimental.pallas import tpu as pltpu
from jax.sharding import PartitionSpec as P

NB = 256
CAP = 20
NZ, NX, NY = 16, 4, 4
NPROW = 2 * NZ
KR = 2
LEVEL = (0, 4, 6, 16)
FAR = NZ // 2
WIDE = NPROW * CAP + NB
SLOT = CAP * 4
STEP = 512
TCH = 4
TROWS = 512 // TCH
BF, F32 = jnp.bfloat16, jnp.float32
VMEM, ANY, SMEM = pltpu.VMEM, pl.ANY, pltpu.SMEM


def spec(space):
    return pl.BlockSpec(memory_space=space)


def remote(src, dst, ss, rs, **where):
    return pltpu.make_async_remote_copy(
        src_ref=src, dst_ref=dst, send_sem=ss, recv_sem=rs,
        device_id=where, device_id_type=pl.DeviceIdType.MESH,
    )


def onehot(cond, value=1.0):
    return jnp.where(cond, value, 0.0).astype(BF)


def column_of(row):
    n = row.shape[1]
    eye = lax.broadcasted_iota(jnp.int32, (n, n), 0) == lax.broadcasted_iota(jnp.int32, (n, n), 1)
    return jnp.sum(jnp.where(eye, jnp.broadcast_to(row, (n, n)), 0), axis=1, keepdims=True)


def owner_of(piv):
    return (piv >> 8) & (NPROW - 1)


def ranks(row, col):
    i0 = lax.broadcasted_iota(jnp.int32, (NB, NB), 0)
    i1 = lax.broadcasted_iota(jnp.int32, (NB, NB), 1)
    before = (owner_of(col) == owner_of(row)) & (i1 < i0) & (row != i1)
    return jnp.dot(onehot(before), jnp.ones((NB, 128), BF), preferred_element_type=F32)


def pick_kernel(later, *refs):
    if later:
        t_ref, row_ref, x_ref, o_ref, most_ref, sem = refs
        first = t_ref[0] * CAP
    else:
        row_ref, x_ref, o_ref, most_ref, sem = refs
        first = 0
    me = lax.axis_index("prow")
    row = row_ref[...]
    col = column_of(row)
    rank = ranks(row, col).astype(jnp.int32)
    ids = lax.broadcasted_iota(jnp.int32, (NB, 128), 0)
    lane = lax.broadcasted_iota(jnp.int32, (NB, 128), 1)
    col = jnp.broadcast_to(col, (NB, 128))
    moved = col != ids
    here = moved & (owner_of(col) == me) & (rank == lane + first)
    local = ((col >> 13) << 8) + (col & 255)
    index = jnp.sum(jnp.where(here, local, 0), axis=0, keepdims=True)
    at = [jnp.sum(jnp.where(lane[:1] == s, index, 0)) for s in range(CAP)]
    most_ref[0] = jnp.max(jnp.where(moved, rank, 0))
    copies = []
    for s in range(CAP):
        src = x_ref.at[(at[s] >> 8) & 7, at[s] & 255]
        copies.append(pltpu.make_async_copy(src, o_ref.at[s], sem.at[s]))
        copies[-1].start()
    for c in copies:
        c.wait()


def pick(trailing, row, t=None):
    later = t is not None
    out, most = pl.pallas_call(
        functools.partial(pick_kernel, later),
        out_shape=(
            jax.ShapeDtypeStruct((CAP, 2, 256), BF),
            jax.ShapeDtypeStruct((1,), jnp.int32),
        ),
        in_specs=[spec(SMEM)] * later + [spec(VMEM), spec(ANY)],
        out_specs=(spec(VMEM), spec(SMEM)),
        scratch_shapes=[pltpu.SemaphoreType.DMA((CAP,))],
        compiler_params=pltpu.CompilerParams(vmem_limit_bytes=16 * 2**20),
        name="pick_later" if later else "pick_rows",
    )(*([t] * later), row, trailing)
    return out.reshape(CAP, 2, 2, 128).transpose(0, 2, 1, 3).reshape(SLOT, 128), most


class Ring:
    def __init__(self, src, slots, zs, zr, ps, pr):
        self.src, self.slots, self.zs, self.zr, self.ps, self.pr = src, slots, zs, zr, ps, pr
        me = lax.axis_index("prow")
        self.z, self.core = me // 2, me % 2

    def rows(self, z, core):
        return self.slots.at[pl.ds(((z % NZ) * 2 + core) * SLOT, SLOT)]

    def to(self, way, hops):
        return ((self.z + NZ + (1 - 2 * way) * hops) % NZ) * 2 + self.core

    def send(self, way, o, hops, src=None):
        dst = self.rows(self.z + NZ - (1 - 2 * way) * (o - hops), self.core)
        c = remote(
            dst if src is None else src, dst, self.zs, self.zr.at[way, o - 1],
            prow=self.to(way, hops),
        )
        c.start()

    def mate(self, offset, src=None):
        dst = self.rows(self.z + NZ + offset, self.core)
        c = remote(
            dst if src is None else src, dst, self.ps, self.pr, prow=self.z * 2 + 1 - self.core
        )
        c.start()

    def begin(self):
        for o in range(KR, 0, -1):
            for way in range(2):
                self.send(way, o, o, self.src)
        self.mate(0, self.src)

    def step(self, o):
        for way in range(2):
            last = FAR - way
            if o > last:
                continue
            dst = self.rows(self.z + NZ - (1 - 2 * way) * o, self.core)
            remote(
                dst, dst, self.zs, self.zr.at[way, o - 1], prow=self.to(0, 0)
            ).wait_recv()
            if o + KR <= last:
                self.send(way, o + KR, KR)
            self.mate(o * (2 * way - 1))

    def finish(self):
        mates = self.slots.at[pl.ds(0, NZ * SLOT)]
        mate = remote(mates, mates, self.ps, self.pr, prow=self.to(0, 0))
        mate.wait_recv()
        mate.wait_send()
        sent = self.slots.at[pl.ds(0, (NZ - 1) * SLOT)]
        remote(sent, sent, self.zs, self.pr, prow=self.to(0, 0)).wait_send()


DMA = pltpu.SemaphoreType.DMA
RING_SEMS = [DMA, DMA((2, FAR)), DMA, DMA]


def greet(ids, meanwhile=None):
    barrier = pltpu.get_barrier_semaphore()
    for where in ids:
        pl.semaphore_signal(barrier, inc=1, device_id=where, device_id_type=pl.DeviceIdType.MESH)
    if meanwhile is not None:
        meanwhile()
    pl.semaphore_wait(barrier, len(ids))


def z_neighbours():
    me = lax.axis_index("prow")
    z, core = me // 2, me % 2
    away = [d for k in range(1, max(KR, 2) + 1) for d in (k, NZ - k)]
    return [{"prow": z * 2 + 1 - core}] + [{"prow": ((z + d) % NZ) * 2 + core} for d in away]


def gather_kernel(src_ref, o_ref, slots, zs, zr, ps, pr, sem):
    greet(z_neighbours())
    ring = Ring(src_ref, slots, zs, zr, ps, pr)
    ring.begin()
    own = pltpu.make_async_copy(src_ref, ring.rows(ring.z, ring.core), sem)
    own.start()
    for s in range(1, FAR + 1):
        ring.step(s)
    own.wait()
    ring.finish()
    o_ref[...] = slots[...]


def gather_round(picked):
    return pl.pallas_call(
        gather_kernel,
        out_shape=jax.ShapeDtypeStruct((NPROW * SLOT, 128), BF),
        in_specs=[spec(VMEM)],
        out_specs=spec(VMEM),
        scratch_shapes=[VMEM((NPROW * SLOT, 128), BF)] + RING_SEMS + [pltpu.SemaphoreType.DMA],
        compiler_params=pltpu.CompilerParams(collective_id=1, has_side_effects=True),
        name="gather_more",
    )(picked)


def later_rounds(trailing, row, most):
    def body(carry):
        t, total = carry
        picked, _ = pick(trailing, row, t.reshape(1))
        rows = gather_round(picked).reshape(NPROW * CAP, 512)
        pivots = row[0] + jnp.minimum(t, 0)
        i = jnp.arange(NB, dtype=jnp.int32)
        owner = owner_of(pivots)
        moved = pivots != i
        before = (owner[:, None] == owner[None, :]) & (i[None, :] < i[:, None]) & moved[None, :]
        at = jnp.sum(before.astype(jnp.int32), axis=1) - t * CAP
        slot = jnp.where(moved & (at >= 0) & (at < CAP), owner * CAP + at, -1)
        chosen = onehot(slot[:, None] == jnp.arange(NPROW * CAP, dtype=jnp.int32)[None, :])
        part = jnp.dot(chosen, rows, preferred_element_type=F32).astype(BF)
        return t + 1, total + part.reshape(NB * 4, 128)

    start = (jnp.int32(1), jnp.zeros((NB * 4, 128), BF))
    return lax.while_loop(lambda c: c[0] * CAP <= most[0], body, start)[1]


class Plane:
    OFF = (0, -1, 1, 2)

    def __init__(self, src, out, ss, rs, last):
        self.src, self.out, self.ss, self.rs, self.last = src, out, ss, rs, last
        q = lax.axis_index("pcol")
        self.x, self.y = q // NY, q % NY

    def device(self, h, first, second):
        dx, dy = (second, first) if h == 0 else (first, second)
        return ((self.x + NX + dx) % NX) * NY + (self.y + NY + dy) % NY

    def part(self, h, first, second, quarter=None):
        base = self.device(h, first, second) * 256 + h * 128
        if quarter is None:
            return self.out.at[pl.ds(base, 128)]
        return self.out.at[pl.ds(base + 64 * quarter, 64)]

    def send(self, h, k, to, ref, src=None):
        rs = self.last if k >= 12 else self.rs.at[h, k]
        remote(ref if src is None else src, ref, self.ss, rs, pcol=to).start()

    def wait(self, h, k, ref):
        remote(ref, ref, self.ss, self.rs.at[h, k], pcol=self.device(h, 0, 0)).wait_recv()

    def second(self, h, m, src=None):
        ref = self.part(h, self.OFF[m], 0)
        self.send(h, 4 + m, self.device(h, 0, 1), ref, src)
        self.send(h, 8 + m, self.device(h, 0, -1), ref, src)

    def begin(self):
        for h in range(2):
            own = self.src.at[pl.ds(h * 128, 128)]
            for k, f in enumerate((2, 1, -1)):
                self.send(h, k, self.device(h, f, 0), self.part(h, 0, 0), own)
        for h in range(2):
            self.second(h, 0, self.src.at[pl.ds(h * 128, 128)])

    def one(self):
        for h in range(2):
            self.wait(h, 1, self.part(h, -1, 0))
            self.second(h, 1)
        for h in range(2):
            self.wait(h, 2, self.part(h, 1, 0))
            self.second(h, 2)

    def two(self):
        for h in range(2):
            self.wait(h, 0, self.part(h, -2, 0))
            self.second(h, 3)

    def three(self, m):
        for h in range(2):
            f = self.OFF[m]
            self.wait(h, 4 + m, self.part(h, f, -1))
            self.send(h, 12 + m, self.device(h, 0, 1), self.part(h, f, -1, 0))
            self.wait(h, 8 + m, self.part(h, f, 1))
            self.send(h, 16 + m, self.device(h, 0, -1), self.part(h, f, 1, 1))

    def four(self):
        got = self.out.at[pl.ds(0, 1024)]
        remote(got, got, self.ss, self.last, pcol=self.device(0, 0, 0)).wait_recv()

    def finish(self):
        sent = self.out.at[pl.ds(0, 3840)]
        remote(sent, sent, self.ss, self.last, pcol=self.device(0, 0, 0)).wait_send()


def plane_neighbours():
    q = lax.axis_index("pcol")
    x, y = q // NY, q % NY
    along_x = [{"pcol": ((x + d) % NX) * NY + y} for d in range(1, NX)]
    return along_x + [{"pcol": x * NY + (y + d) % NY} for d in range(1, NY)]


class Top:
    KINDS = ((0, 2), (1, 2), (0, 1), (1, 1))

    def __init__(self, src, out, ss, rr, ps, pr):
        self.src, self.out, self.ss, self.rr, self.ps, self.pr = src, out, ss, rr, ps, pr
        me = lax.axis_index("prow")
        z = me // 2
        self.z, self.core = z, me % 2
        self.root = me == 0
        self.dist = jnp.where(z <= FAR, z, NZ - z)
        self.relay = z % 2 == 0
        self.goes = (
            self.relay & (z <= FAR - 2),
            self.relay & ((z == 0) | (z >= FAR + 4)),
            self.relay & (z >= FAR + 2),
            self.relay & (((z >= 2) & (z <= FAR)) | (z == FAR + 2)),
        )

    def rows(self, ref, half, n):
        return ref.at[pl.ds(half * 512 + n * TROWS, TROWS)]

    def half(self, half):
        return self.out.at[pl.ds(half * 512, 512)]

    def ring(self, k, n, src):
        way, hops = self.KINDS[k]
        to = ((self.z + NZ + (1 - 2 * way) * hops) % NZ) * 2 + self.core
        return remote(
            self.rows(src, self.core, n), self.rows(self.out, self.core, n),
            self.ss.at[k], self.rr.at[n], prow=to,
        )

    def mate(self, half, n, src, rsem):
        return remote(
            self.rows(src, half, n), self.rows(self.out, half, n),
            self.ps.at[half], rsem, prow=self.z * 2 + 1 - self.core,
        )

    def begin(self):
        @pl.when(self.root)
        def _():
            for n in range(TCH):
                self.mate(1, n, self.src, self.rr.at[n]).start()
                self.ring(0, n, self.src).start()
                self.ring(1, n, self.src).start()
            for n in range(TCH):
                self.mate(0, n, self.src, self.pr).start()

    def own(self, sem):
        return pltpu.make_async_copy(self.src.at[pl.ds(0, 1024)], self.out, sem)

    def step(self, who, chunks):
        @pl.when(who & ~self.root)
        def _():
            for n in chunks:
                self.ring(0, n, self.out).wait_recv()
                for k in range(4):
                    @pl.when(self.goes[k])
                    def _():
                        self.ring(k, n, self.out).start()

                @pl.when(self.z != 0)
                def _():
                    self.mate(self.core, n, self.out, self.pr).start()

    def finish(self):
        other, own = self.half(1 - self.core), self.half(self.core)
        me = self.z * 2 + self.core

        @pl.when(~self.root)
        def _():
            remote(other, other, self.ss.at[0], self.pr, prow=me).wait_recv()

        for k in range(4):
            @pl.when(self.goes[k])
            def _():
                remote(own, own, self.ss.at[k], self.pr, prow=me).wait_send()

        @pl.when(self.z != 0)
        def _():
            remote(own, own, self.ps.at[self.core], self.pr, prow=me).wait_send()

        @pl.when(self.root)
        def _():
            for half in range(2):
                ref = self.half(half)
                remote(ref, ref, self.ps.at[half], self.pr, prow=me).wait_send()


TOP_SEMS = [DMA((4,)), DMA((TCH,)), DMA((2,)), DMA]


def main_kernel(
    x_ref, pick_ref, panel_ref, linv_ref, uinv_ref, row_ref, extra_ref,
    m_ref, xm_ref, st_ref,
    slots, top, panel, panelf, wide, both, chosen, mask,
    zs, zr, zps, zpr, ts, tr, tps, tpr, ss, rs, last, sems,
):
    me = lax.axis_index("prow")
    ring = Ring(pick_ref, slots, zs, zr, zps, zpr)
    plane = Plane(panel_ref, panel, ss, rs, last)
    head = Top(x_ref, top, ts, tr, tps, tpr)
    row = row_ref[...]
    lanes = lax.broadcasted_iota(jnp.int32, (1, NB), 1)
    moved = row != lanes

    def swaps(b):
        rows = lax.broadcasted_iota(jnp.int32, (NB, NB), 0) + (b * NPROW + me) * NB
        hit = (rows == row) & moved
        m_ref[pl.ds(b * NB, NB), NB:] = onehot(hit, -1.0)
        gone = jnp.dot(onehot(hit), jnp.ones((NB, 128), BF), preferred_element_type=F32)
        for j in range(4):
            mask[pl.ds(j, NB, stride=4), :] = gone
        x = x_ref[pl.ds(b * 1024, 1024), :].astype(F32)
        xm_ref[pl.ds(b * 1024, 1024), :] = jnp.where(mask[...] > 0.5, 0.0, x).astype(BF)

    def lower(k):
        piece = panelf[pl.ds((k % 2) * 8 + k // 2, NB, stride=16), :].astype(BF)
        low = lax.dot_general(
            piece, uinv_ref[...], (((0,), (0,)), ((), ())), preferred_element_type=F32
        )
        m_ref[pl.ds(k * 128, 128), :NB] = low.astype(BF)

    def masks():
        for b in range(8):
            swaps(b)

    greet(z_neighbours() + plane_neighbours(), masks)
    ring.begin()
    plane.begin()
    head.begin()
    q = lax.axis_index("pcol")
    own_panel = pltpu.make_async_copy(panel_ref, panel.at[pl.ds(q * 256, 256)], sems.at[0])
    own_panel.start()
    own_slot = pltpu.make_async_copy(pick_ref, ring.rows(ring.z, ring.core), sems.at[1])
    own_slot.start()

    @pl.when(head.root)
    def _():
        head.own(sems.at[2]).start()

    col = column_of(row)
    rank = ranks(row, col).astype(jnp.int32)
    ids = lax.broadcasted_iota(jnp.int32, (NB, 128), 0)
    lane = lax.broadcasted_iota(jnp.int32, (NB, 128), 1)
    goes = jnp.broadcast_to(col, (NB, 128)) != ids
    slot = jnp.where(
        goes & (rank < CAP), owner_of(jnp.broadcast_to(col, (NB, 128))) * CAP + rank, -1
    )
    stay = jnp.where(goes, -1, ids + NPROW * CAP)
    for u in range(WIDE // 128):
        hit = (slot == lane + 128 * u) | (stay == lane + 128 * u)
        chosen[:, 128 * u : 128 * (u + 1)] = onehot(hit)

    near, middle, far = [head.relay & ((head.dist >= LEVEL[k]) & (head.dist < LEVEL[k + 1])) for k in range(3)]
    first, second = range(TCH // 2), range(TCH // 2, TCH)
    ring.step(1)
    ring.step(2)
    plane.one()
    plane.two()
    plane.three(0)
    head.step(near, first)
    ring.step(3)
    ring.step(4)
    head.step(near, second)
    head.step(middle, first)
    plane.three(1)
    plane.three(2)
    ring.step(5)
    ring.step(6)
    head.step(middle, second)
    plane.three(3)
    head.step(far, first)
    ring.step(7)
    ring.step(8)
    head.step(far, second)
    plane.four()
    own_panel.wait()
    panelf[...] = panel[...].astype(F32)
    for k in range(16):
        lower(k)
    head.step(~head.relay, range(TCH))
    own_slot.wait()

    @pl.when(head.root)
    def _():
        head.own(sems.at[2]).wait()

    ring.finish()
    head.finish()
    plane.finish()
    wide[pl.ds(0, NPROW * SLOT), :] = slots[...].astype(F32)
    wide[pl.ds(NPROW * SLOT, 1024), :] = top[...].astype(F32)
    for j in range(4):
        both[:, j * 128 : (j + 1) * 128] = wide[pl.ds(j, WIDE, stride=4), :].astype(BF)
    picked = jnp.dot(chosen[...], both[...], preferred_element_type=F32)
    wide[pl.ds(0, 1024), :] = extra_ref[...].astype(F32)
    more = jnp.concatenate([wide[pl.ds(j, NB, stride=4), :] for j in range(4)], axis=1)
    picked = (picked + more).astype(BF)
    st_ref[pl.ds(0, NB), :] = jnp.dot(
        linv_ref[...], picked, preferred_element_type=F32
    ).astype(BF)
    st_ref[pl.ds(NB, NB), :] = both[pl.ds(NPROW * CAP, NB), :]


def main(tv, picked, pv, linv, uinv, row, extra):
    return pl.pallas_call(
        main_kernel,
        out_shape=(
            jax.ShapeDtypeStruct((8 * NB, 2 * NB), BF),
            jax.ShapeDtypeStruct((8192, 128), BF),
            jax.ShapeDtypeStruct((2 * NB, 2 * NB), BF),
        ),
        in_specs=[spec(VMEM)] * 7,
        out_specs=(spec(VMEM),) * 3,
        scratch_shapes=[
            VMEM((NPROW * SLOT, 128), BF),
            VMEM((1024, 128), BF),
            VMEM((4096, 128), BF),
            VMEM((4096, 128), F32),
            VMEM((4 * WIDE, 128), F32),
            VMEM((WIDE, 512), BF),
            VMEM((NB, WIDE), BF),
            VMEM((1024, 128), F32),
        ]
        + RING_SEMS
        + TOP_SEMS
        + [DMA, DMA((2, 12)), DMA]
        + [DMA((3,))],
        compiler_params=pltpu.CompilerParams(
            collective_id=0, has_side_effects=True, vmem_limit_bytes=40 * 2**20
        ),
        name="gather_prepare",
    )(tv, picked, pv, linv, uinv, row, extra)


def update_kernel(m_ref, xm_ref, st_ref, o_ref, spread, out, sem):
    copies = []
    for i in range(2048 // STEP):
        product = jnp.dot(m_ref[pl.ds(i * STEP, STEP), :], st_ref[...], preferred_element_type=F32)
        for j in range(4):
            spread[i % 2, pl.ds(j, STEP, stride=4), :] = product[:, j * 128 : (j + 1) * 128]
        at = pl.ds(i * STEP * 4, STEP * 4)
        out[at, :] = (xm_ref[at, :].astype(F32) - spread[i % 2]).astype(BF)
        if i == 0:
            @pl.when(lax.axis_index("prow") == 0)
            def _():
                for j in range(4):
                    solved = st_ref[pl.ds(0, NB), j * 128 : (j + 1) * 128]
                    spread[0, pl.ds(j, NB, stride=4), :] = solved.astype(F32)
                out[pl.ds(0, 4 * NB), :] = spread[0, pl.ds(0, 4 * NB), :].astype(BF)

        copies.append(pltpu.make_async_copy(out.at[at], o_ref.at[at], sem.at[i]))
        copies[-1].start()
    for c in copies:
        c.wait()


def update(m, xm, st):
    return pl.pallas_call(
        update_kernel,
        out_shape=jax.ShapeDtypeStruct((8192, 128), BF),
        in_specs=[spec(VMEM)] * 3,
        out_specs=spec(ANY),
        scratch_shapes=[
            VMEM((2, 4 * STEP, 128), F32), VMEM((8192, 128), BF), DMA((2048 // STEP,))
        ],
        compiler_params=pltpu.CompilerParams(vmem_limit_bytes=16 * 2**20),
        name="update",
    )(m, xm, st)


def per_device(trailing, panel, lower_inverse, upper_inverse, pivots):
    tv = trailing.reshape(8, 256, 2, 2, 128).transpose(0, 1, 3, 2, 4).reshape(8192, 128)
    pv = panel.reshape(16, 8, 2, 128).transpose(0, 2, 1, 3).reshape(256, 128)
    row = pivots.reshape(1, NB)
    picked, most = pick(trailing, row)
    extra = later_rounds(trailing, row, most)
    m, xm, st = main(tv, picked, pv, lower_inverse, upper_inverse, row, extra)
    out = update(m, xm, st)
    return out.reshape(8, 256, 2, 2, 128).transpose(0, 1, 3, 2, 4).reshape(trailing.shape)


def solution(mesh):
    placed = (P(None, "prow", None, "pcol"), P("pcol", None, "prow"), P(), P(), P())
    return jax.shard_map(
        per_device,
        mesh=mesh,
        in_specs=placed,
        out_specs=P(None, "prow", None, "pcol"),
        check_vma=False,
    )
```

```python
import functools

import jax
import jax.numpy as jnp
from jax import lax
from jax.experimental import pallas as pl
from jax.experimental.pallas import tpu as pltpu
from jax.sharding import PartitionSpec as P

NB = 256
CAP = 20
NZ, NX, NY = 16, 4, 4
NPROW = 2 * NZ
KR = 2
FAR = NZ // 2
WIDE = NPROW * CAP + NB
SLOT = CAP * 4
STEP = 512
TCH = 4
TROWS = 512 // TCH
BF, F32 = jnp.bfloat16, jnp.float32
VMEM, ANY, SMEM = pltpu.VMEM, pl.ANY, pltpu.SMEM


def spec(space):
    return pl.BlockSpec(memory_space=space)


def remote(src, dst, ss, rs, **where):
    return pltpu.make_async_remote_copy(
        src_ref=src, dst_ref=dst, send_sem=ss, recv_sem=rs,
        device_id=where, device_id_type=pl.DeviceIdType.MESH,
    )


def onehot(cond, value=1.0):
    return jnp.where(cond, value, 0.0).astype(BF)


def column_of(row):
    n = row.shape[1]
    eye = lax.broadcasted_iota(jnp.int32, (n, n), 0) == lax.broadcasted_iota(jnp.int32, (n, n), 1)
    return jnp.sum(jnp.where(eye, jnp.broadcast_to(row, (n, n)), 0), axis=1, keepdims=True)


def owner_of(piv):
    return (piv >> 8) & (NPROW - 1)


def ranks(row, col):
    i0 = lax.broadcasted_iota(jnp.int32, (NB, NB), 0)
    i1 = lax.broadcasted_iota(jnp.int32, (NB, NB), 1)
    before = (owner_of(col) == owner_of(row)) & (i1 < i0) & (row != i1)
    return jnp.dot(onehot(before), jnp.ones((NB, 128), BF), preferred_element_type=F32)


def pick_kernel(later, *refs):
    if later:
        t_ref, row_ref, x_ref, o_ref, most_ref, sem = refs
        first = t_ref[0] * CAP
    else:
        row_ref, x_ref, o_ref, most_ref, sem = refs
        first = 0
    me = lax.axis_index("prow")
    row = row_ref[...]
    col = column_of(row)
    rank = ranks(row, col).astype(jnp.int32)
    ids = lax.broadcasted_iota(jnp.int32, (NB, 128), 0)
    lane = lax.broadcasted_iota(jnp.int32, (NB, 128), 1)
    col = jnp.broadcast_to(col, (NB, 128))
    moved = col != ids
    here = moved & (owner_of(col) == me) & (rank == lane + first)
    local = ((col >> 13) << 8) + (col & 255)
    index = jnp.sum(jnp.where(here, local, 0), axis=0, keepdims=True)
    at = [jnp.sum(jnp.where(lane[:1] == s, index, 0)) for s in range(CAP)]
    most_ref[0] = jnp.max(jnp.where(moved, rank, 0))
    copies = []
    for s in range(CAP):
        src = x_ref.at[(at[s] >> 8) & 7, at[s] & 255]
        copies.append(pltpu.make_async_copy(src, o_ref.at[s], sem.at[s]))
        copies[-1].start()
    for c in copies:
        c.wait()


def pick(trailing, row, t=None):
    later = t is not None
    out, most = pl.pallas_call(
        functools.partial(pick_kernel, later),
        out_shape=(
            jax.ShapeDtypeStruct((CAP, 2, 256), BF),
            jax.ShapeDtypeStruct((1,), jnp.int32),
        ),
        in_specs=[spec(SMEM)] * later + [spec(VMEM), spec(ANY)],
        out_specs=(spec(VMEM), spec(SMEM)),
        scratch_shapes=[pltpu.SemaphoreType.DMA((CAP,))],
        compiler_params=pltpu.CompilerParams(vmem_limit_bytes=16 * 2**20),
        name="pick_later" if later else "pick_rows",
    )(*([t] * later), row, trailing)
    return out.reshape(CAP, 2, 2, 128).transpose(0, 2, 1, 3).reshape(SLOT, 128), most


class Ring:
    def __init__(self, src, slots, zs, zr, ps, pr):
        self.src, self.slots, self.zs, self.zr, self.ps, self.pr = src, slots, zs, zr, ps, pr
        me = lax.axis_index("prow")
        self.z, self.core = me // 2, me % 2

    def rows(self, z, core):
        return self.slots.at[pl.ds(((z % NZ) * 2 + core) * SLOT, SLOT)]

    def to(self, way, hops):
        return ((self.z + NZ + (1 - 2 * way) * hops) % NZ) * 2 + self.core

    def send(self, way, o, hops, src=None):
        dst = self.rows(self.z + NZ - (1 - 2 * way) * (o - hops), self.core)
        c = remote(
            dst if src is None else src, dst, self.zs, self.zr.at[way, o - 1],
            prow=self.to(way, hops),
        )
        c.start()

    def mate(self, offset, src=None):
        dst = self.rows(self.z + NZ + offset, self.core)
        c = remote(
            dst if src is None else src, dst, self.ps, self.pr, prow=self.z * 2 + 1 - self.core
        )
        c.start()

    def begin(self):
        for o in range(KR, 0, -1):
            for way in range(2):
                self.send(way, o, o, self.src)
        self.mate(0, self.src)

    def step(self, o):
        for way in range(2):
            last = FAR - way
            if o > last:
                continue
            dst = self.rows(self.z + NZ - (1 - 2 * way) * o, self.core)
            remote(
                dst, dst, self.zs, self.zr.at[way, o - 1], prow=self.to(0, 0)
            ).wait_recv()
            if o % KR == 0:
                for hops in range(min(KR, last - o), 0, -1):
                    self.send(way, o + hops, hops)
            self.mate(o * (2 * way - 1))

    def finish(self):
        mates = self.slots.at[pl.ds(0, NZ * SLOT)]
        mate = remote(mates, mates, self.ps, self.pr, prow=self.to(0, 0))
        mate.wait_recv()
        mate.wait_send()
        sent = self.slots.at[pl.ds(0, (NZ - 1) * SLOT)]
        remote(sent, sent, self.zs, self.pr, prow=self.to(0, 0)).wait_send()


DMA = pltpu.SemaphoreType.DMA
RING_SEMS = [DMA, DMA((2, FAR)), DMA, DMA]


def greet(ids, meanwhile=None):
    barrier = pltpu.get_barrier_semaphore()
    for where in ids:
        pl.semaphore_signal(barrier, inc=1, device_id=where, device_id_type=pl.DeviceIdType.MESH)
    if meanwhile is not None:
        meanwhile()
    pl.semaphore_wait(barrier, len(ids))


def z_neighbours():
    me = lax.axis_index("prow")
    z, core = me // 2, me % 2
    away = [d for k in sorted({1, 2, 4} | set(range(1, KR + 1))) for d in (k, NZ - k)]
    return [{"prow": z * 2 + 1 - core}] + [{"prow": ((z + d) % NZ) * 2 + core} for d in away]


def gather_kernel(src_ref, o_ref, slots, zs, zr, ps, pr, sem):
    greet(z_neighbours())
    ring = Ring(src_ref, slots, zs, zr, ps, pr)
    ring.begin()
    own = pltpu.make_async_copy(src_ref, ring.rows(ring.z, ring.core), sem)
    own.start()
    for s in range(1, FAR + 1):
        ring.step(s)
    own.wait()
    ring.finish()
    o_ref[...] = slots[...]


def gather_round(picked):
    return pl.pallas_call(
        gather_kernel,
        out_shape=jax.ShapeDtypeStruct((NPROW * SLOT, 128), BF),
        in_specs=[spec(VMEM)],
        out_specs=spec(VMEM),
        scratch_shapes=[VMEM((NPROW * SLOT, 128), BF)] + RING_SEMS + [pltpu.SemaphoreType.DMA],
        compiler_params=pltpu.CompilerParams(collective_id=1, has_side_effects=True),
        name="gather_more",
    )(picked)


def later_rounds(trailing, row, most):
    def body(carry):
        t, total = carry
        picked, _ = pick(trailing, row, t.reshape(1))
        rows = gather_round(picked).reshape(NPROW * CAP, 512)
        pivots = row[0] + jnp.minimum(t, 0)
        i = jnp.arange(NB, dtype=jnp.int32)
        owner = owner_of(pivots)
        moved = pivots != i
        before = (owner[:, None] == owner[None, :]) & (i[None, :] < i[:, None]) & moved[None, :]
        at = jnp.sum(before.astype(jnp.int32), axis=1) - t * CAP
        slot = jnp.where(moved & (at >= 0) & (at < CAP), owner * CAP + at, -1)
        chosen = onehot(slot[:, None] == jnp.arange(NPROW * CAP, dtype=jnp.int32)[None, :])
        part = jnp.dot(chosen, rows, preferred_element_type=F32).astype(BF)
        return t + 1, total + part.reshape(NB * 4, 128)

    start = (jnp.int32(1), jnp.zeros((NB * 4, 128), BF))
    return lax.while_loop(lambda c: c[0] * CAP <= most[0], body, start)[1]


class Plane:
    OFF = (0, -1, 1, 2)

    def __init__(self, src, out, ss, rs, last):
        self.src, self.out, self.ss, self.rs, self.last = src, out, ss, rs, last
        q = lax.axis_index("pcol")
        self.x, self.y = q // NY, q % NY

    def device(self, h, first, second):
        dx, dy = (second, first) if h == 0 else (first, second)
        return ((self.x + NX + dx) % NX) * NY + (self.y + NY + dy) % NY

    def part(self, h, first, second, quarter=None):
        base = self.device(h, first, second) * 256 + h * 128
        if quarter is None:
            return self.out.at[pl.ds(base, 128)]
        return self.out.at[pl.ds(base + 64 * quarter, 64)]

    def send(self, h, k, to, ref, src=None):
        rs = self.last if k >= 12 else self.rs.at[h, k]
        remote(ref if src is None else src, ref, self.ss, rs, pcol=to).start()

    def wait(self, h, k, ref):
        remote(ref, ref, self.ss, self.rs.at[h, k], pcol=self.device(h, 0, 0)).wait_recv()

    def second(self, h, m, src=None):
        ref = self.part(h, self.OFF[m], 0)
        self.send(h, 4 + m, self.device(h, 0, 1), ref, src)
        self.send(h, 8 + m, self.device(h, 0, -1), ref, src)

    def begin(self):
        for h in range(2):
            own = self.src.at[pl.ds(h * 128, 128)]
            for k, f in enumerate((2, 1, -1)):
                self.send(h, k, self.device(h, f, 0), self.part(h, 0, 0), own)
        for h in range(2):
            self.second(h, 0, self.src.at[pl.ds(h * 128, 128)])

    def one(self):
        for h in range(2):
            self.wait(h, 1, self.part(h, -1, 0))
            self.second(h, 1)
        for h in range(2):
            self.wait(h, 2, self.part(h, 1, 0))
            self.second(h, 2)

    def two(self):
        for h in range(2):
            self.wait(h, 0, self.part(h, -2, 0))
            self.second(h, 3)

    def three(self, m):
        for h in range(2):
            f = self.OFF[m]
            self.wait(h, 4 + m, self.part(h, f, -1))
            self.send(h, 12 + m, self.device(h, 0, 1), self.part(h, f, -1, 0))
            self.wait(h, 8 + m, self.part(h, f, 1))
            self.send(h, 16 + m, self.device(h, 0, -1), self.part(h, f, 1, 1))

    def four(self):
        got = self.out.at[pl.ds(0, 1024)]
        remote(got, got, self.ss, self.last, pcol=self.device(0, 0, 0)).wait_recv()

    def finish(self):
        sent = self.out.at[pl.ds(0, 3840)]
        remote(sent, sent, self.ss, self.last, pcol=self.device(0, 0, 0)).wait_send()


def plane_neighbours():
    q = lax.axis_index("pcol")
    x, y = q // NY, q % NY
    along_x = [{"pcol": ((x + d) % NX) * NY + y} for d in range(1, NX)]
    return along_x + [{"pcol": x * NY + (y + d) % NY} for d in range(1, NY)]


class Top:
    KINDS = (4, -4, 1, -1, 2, -2)

    def __init__(self, src, out, ss, rr, ps, pr):
        self.src, self.out, self.ss, self.rr, self.ps, self.pr = src, out, ss, rr, ps, pr
        me = lax.axis_index("prow")
        z = me // 2
        self.z, self.core = z, me % 2
        self.root = me == 0
        self.goes = (
            (z == 0) | (z == 4),
            z == 0,
            (z == 8) | (z == 12) | (z == 14),
            (z == 2) | (z == 4) | (z == 8) | (z == 12),
            (z == 8) | (z == 12),
            (z == 4) | (z == 8),
        )
        self.near = (z == 0) | (z == 4) | (z == 12)
        self.middle = (z == 2) | (z == 8) | (z == 14)
        self.leaf = (z % 4 != 0) & (z != 2) & (z != 14)

    def rows(self, ref, half, n):
        return ref.at[pl.ds(half * 512 + n * TROWS, TROWS)]

    def half(self, half):
        return self.out.at[pl.ds(half * 512, 512)]

    def ring(self, k, n, src):
        to = ((self.z + NZ + self.KINDS[k]) % NZ) * 2 + self.core
        return remote(
            self.rows(src, self.core, n), self.rows(self.out, self.core, n),
            self.ss.at[k], self.rr.at[n], prow=to,
        )

    def mate(self, half, n, src, rsem):
        return remote(
            self.rows(src, half, n), self.rows(self.out, half, n),
            self.ps.at[half], rsem, prow=self.z * 2 + 1 - self.core,
        )

    def begin(self):
        @pl.when(self.root)
        def _():
            for n in range(TCH):
                self.mate(1, n, self.src, self.rr.at[n]).start()
                self.ring(0, n, self.src).start()
                self.ring(1, n, self.src).start()
            for n in range(TCH):
                self.mate(0, n, self.src, self.pr).start()

    def own(self, sem):
        return pltpu.make_async_copy(self.src.at[pl.ds(0, 1024)], self.out, sem)

    def step(self, who, chunks):
        @pl.when(who & ~self.root)
        def _():
            for n in chunks:
                self.ring(0, n, self.out).wait_recv()
                for k in range(6):
                    @pl.when(self.goes[k])
                    def _():
                        self.ring(k, n, self.out).start()

                @pl.when(self.z != 0)
                def _():
                    self.mate(self.core, n, self.out, self.pr).start()

    def late(self):
        @pl.when(self.z == 4)
        def _():
            for n in range(TCH):
                self.ring(2, n, self.out).start()

    def finish(self):
        other, own = self.half(1 - self.core), self.half(self.core)
        me = self.z * 2 + self.core

        @pl.when(~self.root)
        def _():
            remote(other, other, self.ss.at[0], self.pr, prow=me).wait_recv()

        for k in range(6):
            @pl.when(self.goes[k] | (self.z == 4) if k == 2 else self.goes[k])
            def _():
                remote(own, own, self.ss.at[k], self.pr, prow=me).wait_send()

        @pl.when(self.z != 0)
        def _():
            remote(own, own, self.ps.at[self.core], self.pr, prow=me).wait_send()

        @pl.when(self.root)
        def _():
            for half in range(2):
                ref = self.half(half)
                remote(ref, ref, self.ps.at[half], self.pr, prow=me).wait_send()


TOP_SEMS = [DMA((6,)), DMA((TCH,)), DMA((2,)), DMA]


def main_kernel(
    x_ref, pick_ref, panel_ref, linv_ref, uinv_ref, row_ref, extra_ref,
    m_ref, xm_ref, st_ref,
    slots, top, panel, panelf, wide, both, chosen, mask,
    zs, zr, zps, zpr, ts, tr, tps, tpr, ss, rs, last, sems,
):
    me = lax.axis_index("prow")
    ring = Ring(pick_ref, slots, zs, zr, zps, zpr)
    plane = Plane(panel_ref, panel, ss, rs, last)
    head = Top(x_ref, top, ts, tr, tps, tpr)
    row = row_ref[...]
    lanes = lax.broadcasted_iota(jnp.int32, (1, NB), 1)
    moved = row != lanes

    def swaps(b):
        rows = lax.broadcasted_iota(jnp.int32, (NB, NB), 0) + (b * NPROW + me) * NB
        hit = (rows == row) & moved
        m_ref[pl.ds(b * NB, NB), NB:] = onehot(hit, -1.0)
        gone = jnp.dot(onehot(hit), jnp.ones((NB, 128), BF), preferred_element_type=F32)
        for j in range(4):
            mask[pl.ds(j, NB, stride=4), :] = gone
        x = x_ref[pl.ds(b * 1024, 1024), :].astype(F32)
        xm_ref[pl.ds(b * 1024, 1024), :] = jnp.where(mask[...] > 0.5, 0.0, x).astype(BF)

    def lower(k):
        piece = panelf[pl.ds((k % 2) * 8 + k // 2, NB, stride=16), :].astype(BF)
        low = lax.dot_general(
            piece, uinv_ref[...], (((0,), (0,)), ((), ())), preferred_element_type=F32
        )
        m_ref[pl.ds(k * 128, 128), :NB] = low.astype(BF)

    def masks():
        for b in range(8):
            swaps(b)

    greet(z_neighbours() + plane_neighbours(), masks)
    ring.begin()
    plane.begin()
    head.begin()
    q = lax.axis_index("pcol")
    own_panel = pltpu.make_async_copy(panel_ref, panel.at[pl.ds(q * 256, 256)], sems.at[0])
    own_panel.start()
    own_slot = pltpu.make_async_copy(pick_ref, ring.rows(ring.z, ring.core), sems.at[1])
    own_slot.start()

    @pl.when(head.root)
    def _():
        head.own(sems.at[2]).start()

    col = column_of(row)
    rank = ranks(row, col).astype(jnp.int32)
    ids = lax.broadcasted_iota(jnp.int32, (NB, 128), 0)
    lane = lax.broadcasted_iota(jnp.int32, (NB, 128), 1)
    goes = jnp.broadcast_to(col, (NB, 128)) != ids
    slot = jnp.where(
        goes & (rank < CAP), owner_of(jnp.broadcast_to(col, (NB, 128))) * CAP + rank, -1
    )
    stay = jnp.where(goes, -1, ids + NPROW * CAP)
    for u in range(WIDE // 128):
        hit = (slot == lane + 128 * u) | (stay == lane + 128 * u)
        chosen[:, 128 * u : 128 * (u + 1)] = onehot(hit)

    first, second = range(TCH // 2), range(TCH // 2, TCH)
    ring.step(1)
    ring.step(2)
    plane.one()
    plane.two()
    plane.three(0)
    head.step(head.near, first)
    ring.step(3)
    ring.step(4)
    head.step(head.near, second)
    head.late()
    plane.three(1)
    plane.three(2)
    head.step(head.middle, first)
    ring.step(5)
    ring.step(6)
    head.step(head.middle, second)
    plane.three(3)
    ring.step(7)
    ring.step(8)
    plane.four()
    own_panel.wait()
    panelf[...] = panel[...].astype(F32)
    for k in range(16):
        lower(k)
    head.step(head.leaf, range(TCH))
    own_slot.wait()

    @pl.when(head.root)
    def _():
        head.own(sems.at[2]).wait()

    ring.finish()
    head.finish()
    plane.finish()
    wide[pl.ds(0, NPROW * SLOT), :] = slots[...].astype(F32)
    wide[pl.ds(NPROW * SLOT, 1024), :] = top[...].astype(F32)
    for j in range(4):
        both[:, j * 128 : (j + 1) * 128] = wide[pl.ds(j, WIDE, stride=4), :].astype(BF)
    picked = jnp.dot(chosen[...], both[...], preferred_element_type=F32)
    wide[pl.ds(0, 1024), :] = extra_ref[...].astype(F32)
    more = jnp.concatenate([wide[pl.ds(j, NB, stride=4), :] for j in range(4)], axis=1)
    picked = (picked + more).astype(BF)
    st_ref[pl.ds(0, NB), :] = jnp.dot(
        linv_ref[...], picked, preferred_element_type=F32
    ).astype(BF)
    st_ref[pl.ds(NB, NB), :] = both[pl.ds(NPROW * CAP, NB), :]


def main(tv, picked, pv, linv, uinv, row, extra):
    return pl.pallas_call(
        main_kernel,
        out_shape=(
            jax.ShapeDtypeStruct((8 * NB, 2 * NB), BF),
            jax.ShapeDtypeStruct((8192, 128), BF),
            jax.ShapeDtypeStruct((2 * NB, 2 * NB), BF),
        ),
        in_specs=[spec(VMEM)] * 7,
        out_specs=(spec(VMEM),) * 3,
        scratch_shapes=[
            VMEM((NPROW * SLOT, 128), BF),
            VMEM((1024, 128), BF),
            VMEM((4096, 128), BF),
            VMEM((4096, 128), F32),
            VMEM((4 * WIDE, 128), F32),
            VMEM((WIDE, 512), BF),
            VMEM((NB, WIDE), BF),
            VMEM((1024, 128), F32),
        ]
        + RING_SEMS
        + TOP_SEMS
        + [DMA, DMA((2, 12)), DMA]
        + [DMA((3,))],
        compiler_params=pltpu.CompilerParams(
            collective_id=0, has_side_effects=True, vmem_limit_bytes=40 * 2**20
        ),
        name="gather_prepare",
    )(tv, picked, pv, linv, uinv, row, extra)


def update_kernel(m_ref, xm_ref, st_ref, o_ref, spread, out, sem):
    copies = []
    for i in range(2048 // STEP):
        product = jnp.dot(m_ref[pl.ds(i * STEP, STEP), :], st_ref[...], preferred_element_type=F32)
        for j in range(4):
            spread[i % 2, pl.ds(j, STEP, stride=4), :] = product[:, j * 128 : (j + 1) * 128]
        at = pl.ds(i * STEP * 4, STEP * 4)
        out[at, :] = (xm_ref[at, :].astype(F32) - spread[i % 2]).astype(BF)
        if i == 0:
            @pl.when(lax.axis_index("prow") == 0)
            def _():
                for j in range(4):
                    solved = st_ref[pl.ds(0, NB), j * 128 : (j + 1) * 128]
                    spread[0, pl.ds(j, NB, stride=4), :] = solved.astype(F32)
                out[pl.ds(0, 4 * NB), :] = spread[0, pl.ds(0, 4 * NB), :].astype(BF)

        copies.append(pltpu.make_async_copy(out.at[at], o_ref.at[at], sem.at[i]))
        copies[-1].start()
    for c in copies:
        c.wait()


def update(m, xm, st):
    return pl.pallas_call(
        update_kernel,
        out_shape=jax.ShapeDtypeStruct((8192, 128), BF),
        in_specs=[spec(VMEM)] * 3,
        out_specs=spec(ANY),
        scratch_shapes=[
            VMEM((2, 4 * STEP, 128), F32), VMEM((8192, 128), BF), DMA((2048 // STEP,))
        ],
        compiler_params=pltpu.CompilerParams(vmem_limit_bytes=16 * 2**20),
        name="update",
    )(m, xm, st)


def per_device(trailing, panel, lower_inverse, upper_inverse, pivots):
    tv = trailing.reshape(8, 256, 2, 2, 128).transpose(0, 1, 3, 2, 4).reshape(8192, 128)
    pv = panel.reshape(16, 8, 2, 128).transpose(0, 2, 1, 3).reshape(256, 128)
    row = pivots.reshape(1, NB)
    picked, most = pick(trailing, row)
    extra = later_rounds(trailing, row, most)
    m, xm, st = main(tv, picked, pv, lower_inverse, upper_inverse, row, extra)
    out = update(m, xm, st)
    return out.reshape(8, 256, 2, 2, 128).transpose(0, 1, 3, 2, 4).reshape(trailing.shape)


def solution(mesh):
    placed = (P(None, "prow", None, "pcol"), P("pcol", None, "prow"), P(), P(), P())
    return jax.shard_map(
        per_device,
        mesh=mesh,
        in_specs=placed,
        out_specs=P(None, "prow", None, "pcol"),
        check_vma=False,
    )
```

```python
import functools

import jax
import jax.numpy as jnp
from jax import lax
from jax.experimental import pallas as pl
from jax.experimental.pallas import tpu as pltpu
from jax.sharding import PartitionSpec as P

NB = 256
CAP = 20
NZ, NX, NY = 16, 4, 4
NPROW = 2 * NZ
KR = 2
LEVEL = (0, 4, 6, 16)
FAR = NZ // 2
WIDE = NPROW * CAP + NB
SLOT = CAP * 4
STEP = 512
TCH = 4
TROWS = 512 // TCH
BF, F32 = jnp.bfloat16, jnp.float32
VMEM, ANY, SMEM = pltpu.VMEM, pl.ANY, pltpu.SMEM


def spec(space):
    return pl.BlockSpec(memory_space=space)


def remote(src, dst, ss, rs, **where):
    return pltpu.make_async_remote_copy(
        src_ref=src, dst_ref=dst, send_sem=ss, recv_sem=rs,
        device_id=where, device_id_type=pl.DeviceIdType.MESH,
    )


def onehot(cond, value=1.0):
    return jnp.where(cond, value, 0.0).astype(BF)


def column_of(row):
    n = row.shape[1]
    eye = lax.broadcasted_iota(jnp.int32, (n, n), 0) == lax.broadcasted_iota(jnp.int32, (n, n), 1)
    return jnp.sum(jnp.where(eye, jnp.broadcast_to(row, (n, n)), 0), axis=1, keepdims=True)


def owner_of(piv):
    return (piv >> 8) & (NPROW - 1)


def ranks(row, col):
    i0 = lax.broadcasted_iota(jnp.int32, (NB, NB), 0)
    i1 = lax.broadcasted_iota(jnp.int32, (NB, NB), 1)
    before = (owner_of(col) == owner_of(row)) & (i1 < i0) & (row != i1)
    return jnp.dot(onehot(before), jnp.ones((NB, 128), BF), preferred_element_type=F32)


def pick_kernel(later, *refs):
    if later:
        t_ref, row_ref, x_ref, o_ref, most_ref, sem = refs
        first = t_ref[0] * CAP
    else:
        row_ref, x_ref, o_ref, most_ref, sem = refs
        first = 0
    me = lax.axis_index("prow")
    row = row_ref[...]
    col = column_of(row)
    rank = ranks(row, col).astype(jnp.int32)
    ids = lax.broadcasted_iota(jnp.int32, (NB, 128), 0)
    lane = lax.broadcasted_iota(jnp.int32, (NB, 128), 1)
    col = jnp.broadcast_to(col, (NB, 128))
    moved = col != ids
    here = moved & (owner_of(col) == me) & (rank == lane + first)
    local = ((col >> 13) << 8) + (col & 255)
    index = jnp.sum(jnp.where(here, local, 0), axis=0, keepdims=True)
    at = [jnp.sum(jnp.where(lane[:1] == s, index, 0)) for s in range(CAP)]
    most_ref[0] = jnp.max(jnp.where(moved, rank, 0))
    copies = []
    for s in range(CAP):
        src = x_ref.at[(at[s] >> 8) & 7, at[s] & 255]
        copies.append(pltpu.make_async_copy(src, o_ref.at[s], sem.at[s]))
        copies[-1].start()
    for c in copies:
        c.wait()


def pick(trailing, row, t=None):
    later = t is not None
    out, most = pl.pallas_call(
        functools.partial(pick_kernel, later),
        out_shape=(
            jax.ShapeDtypeStruct((CAP, 2, 256), BF),
            jax.ShapeDtypeStruct((1,), jnp.int32),
        ),
        in_specs=[spec(SMEM)] * later + [spec(VMEM), spec(ANY)],
        out_specs=(spec(VMEM), spec(SMEM)),
        scratch_shapes=[pltpu.SemaphoreType.DMA((CAP,))],
        compiler_params=pltpu.CompilerParams(vmem_limit_bytes=16 * 2**20),
        name="pick_later" if later else "pick_rows",
    )(*([t] * later), row, trailing)
    return out.reshape(CAP, 2, 2, 128).transpose(0, 2, 1, 3).reshape(SLOT, 128), most


class Ring:
    def __init__(self, src, slots, zs, zr, ps, pr):
        self.src, self.slots, self.zs, self.zr, self.ps, self.pr = src, slots, zs, zr, ps, pr
        me = lax.axis_index("prow")
        self.z, self.core = me // 2, me % 2

    def rows(self, z, core):
        return self.slots.at[pl.ds(((z % NZ) * 2 + core) * SLOT, SLOT)]

    def to(self, way, hops):
        return ((self.z + NZ + (1 - 2 * way) * hops) % NZ) * 2 + self.core

    def send(self, way, o, hops, src=None):
        dst = self.rows(self.z + NZ - (1 - 2 * way) * (o - hops), self.core)
        c = remote(
            dst if src is None else src, dst, self.zs, self.zr.at[way, o - 1],
            prow=self.to(way, hops),
        )
        c.start()

    def mate(self, offset, src=None):
        dst = self.rows(self.z + NZ + offset, self.core)
        c = remote(
            dst if src is None else src, dst, self.ps, self.pr, prow=self.z * 2 + 1 - self.core
        )
        c.start()

    def begin(self):
        for o in range(KR, 0, -1):
            for way in range(2):
                self.send(way, o, o, self.src)
        self.mate(0, self.src)

    def step(self, o):
        for way in range(2):
            last = FAR - way
            if o > last:
                continue
            dst = self.rows(self.z + NZ - (1 - 2 * way) * o, self.core)
            remote(
                dst, dst, self.zs, self.zr.at[way, o - 1], prow=self.to(0, 0)
            ).wait_recv()
            if o % KR == 0:
                for hops in range(min(KR, last - o), 0, -1):
                    self.send(way, o + hops, hops)
            self.mate(o * (2 * way - 1))

    def finish(self):
        mates = self.slots.at[pl.ds(0, NZ * SLOT)]
        mate = remote(mates, mates, self.ps, self.pr, prow=self.to(0, 0))
        mate.wait_recv()
        mate.wait_send()
        sent = self.slots.at[pl.ds(0, (NZ - 1) * SLOT)]
        remote(sent, sent, self.zs, self.pr, prow=self.to(0, 0)).wait_send()


DMA = pltpu.SemaphoreType.DMA
RING_SEMS = [DMA, DMA((2, FAR)), DMA, DMA]


def greet(ids):
    barrier = pltpu.get_barrier_semaphore()
    for where in ids:
        pl.semaphore_signal(barrier, inc=1, device_id=where, device_id_type=pl.DeviceIdType.MESH)
    pl.semaphore_wait(barrier, len(ids))


def z_neighbours():
    me = lax.axis_index("prow")
    z, core = me // 2, me % 2
    away = [d for k in range(1, max(KR, 2) + 1) for d in (k, NZ - k)]
    return [{"prow": z * 2 + 1 - core}] + [{"prow": ((z + d) % NZ) * 2 + core} for d in away]


def gather_kernel(src_ref, o_ref, slots, zs, zr, ps, pr, sem):
    greet(z_neighbours())
    ring = Ring(src_ref, slots, zs, zr, ps, pr)
    ring.begin()
    own = pltpu.make_async_copy(src_ref, ring.rows(ring.z, ring.core), sem)
    own.start()
    for s in range(1, FAR + 1):
        ring.step(s)
    own.wait()
    ring.finish()
    o_ref[...] = slots[...]


def gather_round(picked):
    return pl.pallas_call(
        gather_kernel,
        out_shape=jax.ShapeDtypeStruct((NPROW * SLOT, 128), BF),
        in_specs=[spec(VMEM)],
        out_specs=spec(VMEM),
        scratch_shapes=[VMEM((NPROW * SLOT, 128), BF)] + RING_SEMS + [pltpu.SemaphoreType.DMA],
        compiler_params=pltpu.CompilerParams(collective_id=1, has_side_effects=True),
        name="gather_more",
    )(picked)


def later_rounds(trailing, row, most):
    def body(carry):
        t, total = carry
        picked, _ = pick(trailing, row, t.reshape(1))
        rows = gather_round(picked).reshape(NPROW * CAP, 512)
        pivots = row[0] + jnp.minimum(t, 0)
        i = jnp.arange(NB, dtype=jnp.int32)
        owner = owner_of(pivots)
        moved = pivots != i
        before = (owner[:, None] == owner[None, :]) & (i[None, :] < i[:, None]) & moved[None, :]
        at = jnp.sum(before.astype(jnp.int32), axis=1) - t * CAP
        slot = jnp.where(moved & (at >= 0) & (at < CAP), owner * CAP + at, -1)
        chosen = onehot(slot[:, None] == jnp.arange(NPROW * CAP, dtype=jnp.int32)[None, :])
        part = jnp.dot(chosen, rows, preferred_element_type=F32).astype(BF)
        return t + 1, total + part.reshape(NB * 4, 128)

    start = (jnp.int32(1), jnp.zeros((NB * 4, 128), BF))
    return lax.while_loop(lambda c: c[0] * CAP <= most[0], body, start)[1]


class Plane:
    OFF = (0, -1, 1, 2)

    def __init__(self, src, out, ss, rs, last):
        self.src, self.out, self.ss, self.rs, self.last = src, out, ss, rs, last
        q = lax.axis_index("pcol")
        self.x, self.y = q // NY, q % NY

    def device(self, h, first, second):
        dx, dy = (second, first) if h == 0 else (first, second)
        return ((self.x + NX + dx) % NX) * NY + (self.y + NY + dy) % NY

    def part(self, h, first, second, quarter=None):
        base = self.device(h, first, second) * 256 + h * 128
        if quarter is None:
            return self.out.at[pl.ds(base, 128)]
        return self.out.at[pl.ds(base + 64 * quarter, 64)]

    def send(self, h, k, to, ref, src=None):
        rs = self.last if k >= 12 else self.rs.at[h, k]
        remote(ref if src is None else src, ref, self.ss, rs, pcol=to).start()

    def wait(self, h, k, ref):
        remote(ref, ref, self.ss, self.rs.at[h, k], pcol=self.device(h, 0, 0)).wait_recv()

    def second(self, h, m, src=None):
        ref = self.part(h, self.OFF[m], 0)
        self.send(h, 4 + m, self.device(h, 0, 1), ref, src)
        self.send(h, 8 + m, self.device(h, 0, -1), ref, src)

    def begin(self):
        for h in range(2):
            own = self.src.at[pl.ds(h * 128, 128)]
            for k, f in enumerate((2, 1, -1)):
                self.send(h, k, self.device(h, f, 0), self.part(h, 0, 0), own)
        for h in range(2):
            self.second(h, 0, self.src.at[pl.ds(h * 128, 128)])

    def one(self):
        for h in range(2):
            self.wait(h, 1, self.part(h, -1, 0))
            self.second(h, 1)
        for h in range(2):
            self.wait(h, 2, self.part(h, 1, 0))
            self.second(h, 2)

    def two(self):
        for h in range(2):
            self.wait(h, 0, self.part(h, -2, 0))
            self.second(h, 3)

    def three(self, m):
        for h in range(2):
            f = self.OFF[m]
            self.wait(h, 4 + m, self.part(h, f, -1))
            self.send(h, 12 + m, self.device(h, 0, 1), self.part(h, f, -1, 0))
            self.wait(h, 8 + m, self.part(h, f, 1))
            self.send(h, 16 + m, self.device(h, 0, -1), self.part(h, f, 1, 1))

    def four(self):
        got = self.out.at[pl.ds(0, 1024)]
        remote(got, got, self.ss, self.last, pcol=self.device(0, 0, 0)).wait_recv()

    def finish(self):
        sent = self.out.at[pl.ds(0, 3840)]
        remote(sent, sent, self.ss, self.last, pcol=self.device(0, 0, 0)).wait_send()


def plane_neighbours():
    q = lax.axis_index("pcol")
    x, y = q // NY, q % NY
    along_x = [{"pcol": ((x + d) % NX) * NY + y} for d in range(1, NX)]
    return along_x + [{"pcol": x * NY + (y + d) % NY} for d in range(1, NY)]


class Top:
    KINDS = ((0, 2), (1, 2), (0, 1), (1, 1))

    def __init__(self, src, out, ss, rr, ps, pr):
        self.src, self.out, self.ss, self.rr, self.ps, self.pr = src, out, ss, rr, ps, pr
        me = lax.axis_index("prow")
        z = me // 2
        self.z, self.core = z, me % 2
        self.root = me == 0
        self.dist = jnp.where(z <= FAR, z, NZ - z)
        self.relay = z % 2 == 0
        self.goes = (
            self.relay & (z <= FAR - 2),
            self.relay & ((z == 0) | (z >= FAR + 4)),
            self.relay & (z >= FAR + 2),
            self.relay & (((z >= 2) & (z <= FAR)) | (z == FAR + 2)),
        )

    def rows(self, ref, half, n):
        return ref.at[pl.ds(half * 512 + n * TROWS, TROWS)]

    def half(self, half):
        return self.out.at[pl.ds(half * 512, 512)]

    def ring(self, k, n, src):
        way, hops = self.KINDS[k]
        to = ((self.z + NZ + (1 - 2 * way) * hops) % NZ) * 2 + self.core
        return remote(
            self.rows(src, self.core, n), self.rows(self.out, self.core, n),
            self.ss.at[k], self.rr.at[n], prow=to,
        )

    def mate(self, half, n, src, rsem):
        return remote(
            self.rows(src, half, n), self.rows(self.out, half, n),
            self.ps.at[half], rsem, prow=self.z * 2 + 1 - self.core,
        )

    def begin(self):
        @pl.when(self.root)
        def _():
            for n in range(TCH):
                self.mate(1, n, self.src, self.rr.at[n]).start()
                self.ring(0, n, self.src).start()
                self.ring(1, n, self.src).start()
            for n in range(TCH):
                self.mate(0, n, self.src, self.pr).start()

    def own(self, sem):
        return pltpu.make_async_copy(self.src.at[pl.ds(0, 1024)], self.out, sem)

    def step(self, who, chunks):
        @pl.when(who & ~self.root)
        def _():
            for n in chunks:
                self.ring(0, n, self.out).wait_recv()
                for k in range(4):
                    @pl.when(self.goes[k])
                    def _():
                        self.ring(k, n, self.out).start()

                @pl.when(self.z != 0)
                def _():
                    self.mate(self.core, n, self.out, self.pr).start()

    def finish(self):
        other, own = self.half(1 - self.core), self.half(self.core)
        me = self.z * 2 + self.core

        @pl.when(~self.root)
        def _():
            remote(other, other, self.ss.at[0], self.pr, prow=me).wait_recv()

        for k in range(4):
            @pl.when(self.goes[k])
            def _():
                remote(own, own, self.ss.at[k], self.pr, prow=me).wait_send()

        @pl.when(self.z != 0)
        def _():
            remote(own, own, self.ps.at[self.core], self.pr, prow=me).wait_send()

        @pl.when(self.root)
        def _():
            for half in range(2):
                ref = self.half(half)
                remote(ref, ref, self.ps.at[half], self.pr, prow=me).wait_send()


TOP_SEMS = [DMA((4,)), DMA((TCH,)), DMA((2,)), DMA]


def main_kernel(
    x_ref, pick_ref, panel_ref, linv_ref, uinv_ref, row_ref, extra_ref,
    m_ref, xm_ref, st_ref,
    slots, top, panel, panelf, wide, both, chosen, mask,
    zs, zr, zps, zpr, ts, tr, tps, tpr, ss, rs, last, sems,
):
    me = lax.axis_index("prow")
    ring = Ring(pick_ref, slots, zs, zr, zps, zpr)
    plane = Plane(panel_ref, panel, ss, rs, last)
    head = Top(x_ref, top, ts, tr, tps, tpr)
    row = row_ref[...]
    lanes = lax.broadcasted_iota(jnp.int32, (1, NB), 1)
    moved = row != lanes

    def swaps(b):
        rows = lax.broadcasted_iota(jnp.int32, (NB, NB), 0) + (b * NPROW + me) * NB
        hit = (rows == row) & moved
        m_ref[pl.ds(b * NB, NB), NB:] = onehot(hit, -1.0)
        gone = jnp.dot(onehot(hit), jnp.ones((NB, 128), BF), preferred_element_type=F32)
        for j in range(4):
            mask[pl.ds(j, NB, stride=4), :] = gone
        x = x_ref[pl.ds(b * 1024, 1024), :].astype(F32)
        xm_ref[pl.ds(b * 1024, 1024), :] = jnp.where(mask[...] > 0.5, 0.0, x).astype(BF)

    def lower(k):
        piece = panelf[pl.ds((k % 2) * 8 + k // 2, NB, stride=16), :].astype(BF)
        low = lax.dot_general(
            piece, uinv_ref[...], (((0,), (0,)), ((), ())), preferred_element_type=F32
        )
        m_ref[pl.ds(k * 128, 128), :NB] = low.astype(BF)

    greet(z_neighbours() + plane_neighbours())
    ring.begin()
    plane.begin()
    head.begin()
    q = lax.axis_index("pcol")
    own_panel = pltpu.make_async_copy(panel_ref, panel.at[pl.ds(q * 256, 256)], sems.at[0])
    own_panel.start()
    own_slot = pltpu.make_async_copy(pick_ref, ring.rows(ring.z, ring.core), sems.at[1])
    own_slot.start()

    @pl.when(head.root)
    def _():
        head.own(sems.at[2]).start()

    col = column_of(row)
    rank = ranks(row, col).astype(jnp.int32)
    ids = lax.broadcasted_iota(jnp.int32, (NB, 128), 0)
    lane = lax.broadcasted_iota(jnp.int32, (NB, 128), 1)
    goes = jnp.broadcast_to(col, (NB, 128)) != ids
    slot = jnp.where(
        goes & (rank < CAP), owner_of(jnp.broadcast_to(col, (NB, 128))) * CAP + rank, -1
    )
    stay = jnp.where(goes, -1, ids + NPROW * CAP)
    for u in range(WIDE // 128):
        hit = (slot == lane + 128 * u) | (stay == lane + 128 * u)
        chosen[:, 128 * u : 128 * (u + 1)] = onehot(hit)

    for b in range(8):
        swaps(b)

    near, middle, far = [
        head.relay & ((head.dist >= LEVEL[k]) & (head.dist < LEVEL[k + 1])) for k in range(3)
    ]
    first, second = range(TCH // 2), range(TCH // 2, TCH)
    ring.step(1)
    ring.step(2)
    plane.one()
    plane.two()
    plane.three(0)
    head.step(near, first)
    ring.step(3)
    ring.step(4)
    head.step(near, second)
    head.step(middle, first)
    plane.three(1)
    plane.three(2)
    ring.step(5)
    ring.step(6)
    head.step(middle, second)
    plane.three(3)
    head.step(far, range(TCH))
    plane.four()
    own_panel.wait()
    panelf[...] = panel[...].astype(F32)
    for k in range(16):
        lower(k)
    head.step(~head.relay, range(TCH))
    ring.step(7)
    ring.step(8)

    @pl.when(head.root)
    def _():
        head.own(sems.at[2]).wait()

    head.finish()
    plane.finish()
    wide[pl.ds(NPROW * SLOT, 1024), :] = top[...].astype(F32)
    for j in range(4):
        both[pl.ds(NPROW * CAP, NB), j * 128 : (j + 1) * 128] = wide[
            pl.ds(NPROW * SLOT + j, NB, stride=4), :
        ].astype(BF)
    st_ref[pl.ds(NB, NB), :] = both[pl.ds(NPROW * CAP, NB), :]
    own_slot.wait()
    ring.finish()
    wide[pl.ds(0, NPROW * SLOT), :] = slots[...].astype(F32)
    for j in range(4):
        both[pl.ds(0, NPROW * CAP), j * 128 : (j + 1) * 128] = wide[
            pl.ds(j, NPROW * CAP, stride=4), :
        ].astype(BF)
    picked = jnp.dot(chosen[...], both[...], preferred_element_type=F32)
    wide[pl.ds(0, 1024), :] = extra_ref[...].astype(F32)
    more = jnp.concatenate([wide[pl.ds(j, NB, stride=4), :] for j in range(4)], axis=1)
    picked = (picked + more).astype(BF)
    st_ref[pl.ds(0, NB), :] = jnp.dot(
        linv_ref[...], picked, preferred_element_type=F32
    ).astype(BF)


def main(tv, picked, pv, linv, uinv, row, extra):
    return pl.pallas_call(
        main_kernel,
        out_shape=(
            jax.ShapeDtypeStruct((8 * NB, 2 * NB), BF),
            jax.ShapeDtypeStruct((8192, 128), BF),
            jax.ShapeDtypeStruct((2 * NB, 2 * NB), BF),
        ),
        in_specs=[spec(VMEM)] * 7,
        out_specs=(spec(VMEM),) * 3,
        scratch_shapes=[
            VMEM((NPROW * SLOT, 128), BF),
            VMEM((1024, 128), BF),
            VMEM((4096, 128), BF),
            VMEM((4096, 128), F32),
            VMEM((4 * WIDE, 128), F32),
            VMEM((WIDE, 512), BF),
            VMEM((NB, WIDE), BF),
            VMEM((1024, 128), F32),
        ]
        + RING_SEMS
        + TOP_SEMS
        + [DMA, DMA((2, 12)), DMA]
        + [DMA((3,))],
        compiler_params=pltpu.CompilerParams(
            collective_id=0, has_side_effects=True, vmem_limit_bytes=40 * 2**20
        ),
        name="gather_prepare",
    )(tv, picked, pv, linv, uinv, row, extra)


def update_kernel(m_ref, xm_ref, st_ref, o_ref, spread, out, sem):
    copies = []
    for i in range(2048 // STEP):
        product = jnp.dot(m_ref[pl.ds(i * STEP, STEP), :], st_ref[...], preferred_element_type=F32)
        for j in range(4):
            spread[i % 2, pl.ds(j, STEP, stride=4), :] = product[:, j * 128 : (j + 1) * 128]
        at = pl.ds(i * STEP * 4, STEP * 4)
        out[at, :] = (xm_ref[at, :].astype(F32) - spread[i % 2]).astype(BF)
        if i == 0:
            @pl.when(lax.axis_index("prow") == 0)
            def _():
                for j in range(4):
                    solved = st_ref[pl.ds(0, NB), j * 128 : (j + 1) * 128]
                    spread[0, pl.ds(j, NB, stride=4), :] = solved.astype(F32)
                out[pl.ds(0, 4 * NB), :] = spread[0, pl.ds(0, 4 * NB), :].astype(BF)

        copies.append(pltpu.make_async_copy(out.at[at], o_ref.at[at], sem.at[i]))
        copies[-1].start()
    for c in copies:
        c.wait()


def update(m, xm, st):
    return pl.pallas_call(
        update_kernel,
        out_shape=jax.ShapeDtypeStruct((8192, 128), BF),
        in_specs=[spec(VMEM)] * 3,
        out_specs=spec(ANY),
        scratch_shapes=[
            VMEM((2, 4 * STEP, 128), F32), VMEM((8192, 128), BF), DMA((2048 // STEP,))
        ],
        compiler_params=pltpu.CompilerParams(vmem_limit_bytes=16 * 2**20),
        name="update",
    )(m, xm, st)


def per_device(trailing, panel, lower_inverse, upper_inverse, pivots):
    tv = trailing.reshape(8, 256, 2, 2, 128).transpose(0, 1, 3, 2, 4).reshape(8192, 128)
    pv = panel.reshape(16, 8, 2, 128).transpose(0, 2, 1, 3).reshape(256, 128)
    row = pivots.reshape(1, NB)
    picked, most = pick(trailing, row)
    extra = later_rounds(trailing, row, most)
    m, xm, st = main(tv, picked, pv, lower_inverse, upper_inverse, row, extra)
    out = update(m, xm, st)
    return out.reshape(8, 256, 2, 2, 128).transpose(0, 1, 3, 2, 4).reshape(trailing.shape)


def solution(mesh):
    placed = (P(None, "prow", None, "pcol"), P("pcol", None, "prow"), P(), P(), P())
    return jax.shard_map(
        per_device,
        mesh=mesh,
        in_specs=placed,
        out_specs=P(None, "prow", None, "pcol"),
        check_vma=False,
    )
```

```python
import functools

import jax
import jax.numpy as jnp
from jax import lax
from jax.experimental import pallas as pl
from jax.experimental.pallas import tpu as pltpu
from jax.sharding import PartitionSpec as P

NB = 256
CAP = 20
NZ, NX, NY = 16, 4, 4
NPROW = 2 * NZ
KR = 3
LEVEL = (0, 4, 6, 16)
FAR = NZ // 2
WIDE = NPROW * CAP + NB
SLOT = CAP * 4
STEP = 512
TCH = 4
TROWS = 512 // TCH
BF, F32 = jnp.bfloat16, jnp.float32
VMEM, ANY, SMEM = pltpu.VMEM, pl.ANY, pltpu.SMEM


def spec(space):
    return pl.BlockSpec(memory_space=space)


def remote(src, dst, ss, rs, **where):
    return pltpu.make_async_remote_copy(
        src_ref=src, dst_ref=dst, send_sem=ss, recv_sem=rs,
        device_id=where, device_id_type=pl.DeviceIdType.MESH,
    )


def onehot(cond, value=1.0):
    return jnp.where(cond, value, 0.0).astype(BF)


def column_of(row):
    n = row.shape[1]
    eye = lax.broadcasted_iota(jnp.int32, (n, n), 0) == lax.broadcasted_iota(jnp.int32, (n, n), 1)
    return jnp.sum(jnp.where(eye, jnp.broadcast_to(row, (n, n)), 0), axis=1, keepdims=True)


def owner_of(piv):
    return (piv >> 8) & (NPROW - 1)


def ranks(row, col):
    i0 = lax.broadcasted_iota(jnp.int32, (NB, NB), 0)
    i1 = lax.broadcasted_iota(jnp.int32, (NB, NB), 1)
    before = (owner_of(col) == owner_of(row)) & (i1 < i0) & (row != i1)
    return jnp.dot(onehot(before), jnp.ones((NB, 128), BF), preferred_element_type=F32)


def pick_kernel(later, *refs):
    if later:
        t_ref, row_ref, x_ref, o_ref, most_ref, sem = refs
        first = t_ref[0] * CAP
    else:
        row_ref, x_ref, o_ref, most_ref, sem = refs
        first = 0
    me = lax.axis_index("prow")
    row = row_ref[...]
    col = column_of(row)
    rank = ranks(row, col).astype(jnp.int32)
    ids = lax.broadcasted_iota(jnp.int32, (NB, 128), 0)
    lane = lax.broadcasted_iota(jnp.int32, (NB, 128), 1)
    col = jnp.broadcast_to(col, (NB, 128))
    moved = col != ids
    here = moved & (owner_of(col) == me) & (rank == lane + first)
    local = ((col >> 13) << 8) + (col & 255)
    index = jnp.sum(jnp.where(here, local, 0), axis=0, keepdims=True)
    at = [jnp.sum(jnp.where(lane[:1] == s, index, 0)) for s in range(CAP)]
    most_ref[0] = jnp.max(jnp.where(moved, rank, 0))
    copies = []
    for s in range(CAP):
        src = x_ref.at[(at[s] >> 8) & 7, at[s] & 255]
        copies.append(pltpu.make_async_copy(src, o_ref.at[s], sem.at[s]))
        copies[-1].start()
    for c in copies:
        c.wait()


def pick(trailing, row, t=None):
    later = t is not None
    out, most = pl.pallas_call(
        functools.partial(pick_kernel, later),
        out_shape=(
            jax.ShapeDtypeStruct((CAP, 2, 256), BF),
            jax.ShapeDtypeStruct((1,), jnp.int32),
        ),
        in_specs=[spec(SMEM)] * later + [spec(VMEM), spec(ANY)],
        out_specs=(spec(VMEM), spec(SMEM)),
        scratch_shapes=[pltpu.SemaphoreType.DMA((CAP,))],
        compiler_params=pltpu.CompilerParams(vmem_limit_bytes=16 * 2**20),
        name="pick_later" if later else "pick_rows",
    )(*([t] * later), row, trailing)
    return out.reshape(CAP, 2, 2, 128).transpose(0, 2, 1, 3).reshape(SLOT, 128), most


class Ring:
    def __init__(self, src, slots, zs, zr, ps, pr):
        self.src, self.slots, self.zs, self.zr, self.ps, self.pr = src, slots, zs, zr, ps, pr
        me = lax.axis_index("prow")
        self.z, self.core = me // 2, me % 2

    def rows(self, z, core):
        return self.slots.at[pl.ds(((z % NZ) * 2 + core) * SLOT, SLOT)]

    def to(self, way, hops):
        return ((self.z + NZ + (1 - 2 * way) * hops) % NZ) * 2 + self.core

    def send(self, way, o, hops, src=None):
        dst = self.rows(self.z + NZ - (1 - 2 * way) * (o - hops), self.core)
        c = remote(
            dst if src is None else src, dst, self.zs, self.zr.at[way, o - 1],
            prow=self.to(way, hops),
        )
        c.start()

    def mate(self, offset, src=None):
        dst = self.rows(self.z + NZ + offset, self.core)
        c = remote(
            dst if src is None else src, dst, self.ps, self.pr, prow=self.z * 2 + 1 - self.core
        )
        c.start()

    def begin(self):
        for o in range(KR, 0, -1):
            for way in range(2):
                self.send(way, o, o, self.src)
        self.mate(0, self.src)

    def step(self, o):
        for way in range(2):
            last = FAR - way
            if o > last:
                continue
            dst = self.rows(self.z + NZ - (1 - 2 * way) * o, self.core)
            remote(
                dst, dst, self.zs, self.zr.at[way, o - 1], prow=self.to(0, 0)
            ).wait_recv()
            if o % KR == 0:
                for hops in range(min(KR, last - o), 0, -1):
                    self.send(way, o + hops, hops)
            self.mate(o * (2 * way - 1))

    def finish(self):
        mates = self.slots.at[pl.ds(0, NZ * SLOT)]
        mate = remote(mates, mates, self.ps, self.pr, prow=self.to(0, 0))
        mate.wait_recv()
        mate.wait_send()
        sent = self.slots.at[pl.ds(0, (NZ - 1) * SLOT)]
        remote(sent, sent, self.zs, self.pr, prow=self.to(0, 0)).wait_send()


DMA = pltpu.SemaphoreType.DMA
RING_SEMS = [DMA, DMA((2, FAR)), DMA, DMA]


def greet(ids):
    barrier = pltpu.get_barrier_semaphore()
    for where in ids:
        pl.semaphore_signal(barrier, inc=1, device_id=where, device_id_type=pl.DeviceIdType.MESH)
    pl.semaphore_wait(barrier, len(ids))


def z_neighbours():
    me = lax.axis_index("prow")
    z, core = me // 2, me % 2
    away = [d for k in range(1, max(KR, 2) + 1) for d in (k, NZ - k)]
    return [{"prow": z * 2 + 1 - core}] + [{"prow": ((z + d) % NZ) * 2 + core} for d in away]


def gather_kernel(src_ref, o_ref, slots, zs, zr, ps, pr, sem):
    greet(z_neighbours())
    ring = Ring(src_ref, slots, zs, zr, ps, pr)
    ring.begin()
    own = pltpu.make_async_copy(src_ref, ring.rows(ring.z, ring.core), sem)
    own.start()
    for s in range(1, FAR + 1):
        ring.step(s)
    own.wait()
    ring.finish()
    o_ref[...] = slots[...]


def gather_round(picked):
    return pl.pallas_call(
        gather_kernel,
        out_shape=jax.ShapeDtypeStruct((NPROW * SLOT, 128), BF),
        in_specs=[spec(VMEM)],
        out_specs=spec(VMEM),
        scratch_shapes=[VMEM((NPROW * SLOT, 128), BF)] + RING_SEMS + [pltpu.SemaphoreType.DMA],
        compiler_params=pltpu.CompilerParams(collective_id=1, has_side_effects=True),
        name="gather_more",
    )(picked)


def later_rounds(trailing, row, most):
    def body(carry):
        t, total = carry
        picked, _ = pick(trailing, row, t.reshape(1))
        rows = gather_round(picked).reshape(NPROW * CAP, 512)
        pivots = row[0] + jnp.minimum(t, 0)
        i = jnp.arange(NB, dtype=jnp.int32)
        owner = owner_of(pivots)
        moved = pivots != i
        before = (owner[:, None] == owner[None, :]) & (i[None, :] < i[:, None]) & moved[None, :]
        at = jnp.sum(before.astype(jnp.int32), axis=1) - t * CAP
        slot = jnp.where(moved & (at >= 0) & (at < CAP), owner * CAP + at, -1)
        chosen = onehot(slot[:, None] == jnp.arange(NPROW * CAP, dtype=jnp.int32)[None, :])
        part = jnp.dot(chosen, rows, preferred_element_type=F32).astype(BF)
        return t + 1, total + part.reshape(NB * 4, 128)

    start = (jnp.int32(1), jnp.zeros((NB * 4, 128), BF))
    return lax.while_loop(lambda c: c[0] * CAP <= most[0], body, start)[1]


class Plane:
    OFF = (0, -1, 1, 2)

    def __init__(self, src, out, ss, rs, last):
        self.src, self.out, self.ss, self.rs, self.last = src, out, ss, rs, last
        q = lax.axis_index("pcol")
        self.x, self.y = q // NY, q % NY

    def device(self, h, first, second):
        dx, dy = (second, first) if h == 0 else (first, second)
        return ((self.x + NX + dx) % NX) * NY + (self.y + NY + dy) % NY

    def part(self, h, first, second, quarter=None):
        base = self.device(h, first, second) * 256 + h * 128
        if quarter is None:
            return self.out.at[pl.ds(base, 128)]
        return self.out.at[pl.ds(base + 64 * quarter, 64)]

    def send(self, h, k, to, ref, src=None):
        rs = self.last if k >= 12 else self.rs.at[h, k]
        remote(ref if src is None else src, ref, self.ss, rs, pcol=to).start()

    def wait(self, h, k, ref):
        remote(ref, ref, self.ss, self.rs.at[h, k], pcol=self.device(h, 0, 0)).wait_recv()

    def second(self, h, m, src=None):
        ref = self.part(h, self.OFF[m], 0)
        self.send(h, 4 + m, self.device(h, 0, 1), ref, src)
        self.send(h, 8 + m, self.device(h, 0, -1), ref, src)

    def begin(self):
        for h in range(2):
            own = self.src.at[pl.ds(h * 128, 128)]
            for k, f in enumerate((2, 1, -1)):
                self.send(h, k, self.device(h, f, 0), self.part(h, 0, 0), own)
        for h in range(2):
            self.second(h, 0, self.src.at[pl.ds(h * 128, 128)])

    def one(self):
        for h in range(2):
            self.wait(h, 1, self.part(h, -1, 0))
            self.second(h, 1)
        for h in range(2):
            self.wait(h, 2, self.part(h, 1, 0))
            self.second(h, 2)

    def two(self):
        for h in range(2):
            self.wait(h, 0, self.part(h, -2, 0))
            self.second(h, 3)

    def three(self, m):
        for h in range(2):
            f = self.OFF[m]
            self.wait(h, 4 + m, self.part(h, f, -1))
            self.send(h, 12 + m, self.device(h, 0, 1), self.part(h, f, -1, 0))
            self.wait(h, 8 + m, self.part(h, f, 1))
            self.send(h, 16 + m, self.device(h, 0, -1), self.part(h, f, 1, 1))

    def four(self):
        got = self.out.at[pl.ds(0, 1024)]
        remote(got, got, self.ss, self.last, pcol=self.device(0, 0, 0)).wait_recv()

    def finish(self):
        sent = self.out.at[pl.ds(0, 3840)]
        remote(sent, sent, self.ss, self.last, pcol=self.device(0, 0, 0)).wait_send()


def plane_neighbours():
    q = lax.axis_index("pcol")
    x, y = q // NY, q % NY
    along_x = [{"pcol": ((x + d) % NX) * NY + y} for d in range(1, NX)]
    return along_x + [{"pcol": x * NY + (y + d) % NY} for d in range(1, NY)]


class Top:
    KINDS = ((0, 2), (1, 2), (0, 1), (1, 1))

    def __init__(self, src, out, ss, rr, ps, pr):
        self.src, self.out, self.ss, self.rr, self.ps, self.pr = src, out, ss, rr, ps, pr
        me = lax.axis_index("prow")
        z = me // 2
        self.z, self.core = z, me % 2
        self.root = me == 0
        self.dist = jnp.where(z <= FAR, z, NZ - z)
        self.relay = z % 2 == 0
        self.goes = (
            self.relay & (z <= FAR - 2),
            self.relay & ((z == 0) | (z >= FAR + 4)),
            self.relay & (z >= FAR + 2),
            self.relay & (((z >= 2) & (z <= FAR)) | (z == FAR + 2)),
        )

    def rows(self, ref, half, n):
        return ref.at[pl.ds(half * 512 + n * TROWS, TROWS)]

    def half(self, half):
        return self.out.at[pl.ds(half * 512, 512)]

    def ring(self, k, n, src):
        way, hops = self.KINDS[k]
        to = ((self.z + NZ + (1 - 2 * way) * hops) % NZ) * 2 + self.core
        return remote(
            self.rows(src, self.core, n), self.rows(self.out, self.core, n),
            self.ss.at[k], self.rr.at[n], prow=to,
        )

    def mate(self, half, n, src, rsem):
        return remote(
            self.rows(src, half, n), self.rows(self.out, half, n),
            self.ps.at[half], rsem, prow=self.z * 2 + 1 - self.core,
        )

    def begin(self):
        @pl.when(self.root)
        def _():
            for n in range(TCH):
                self.mate(1, n, self.src, self.rr.at[n]).start()
                self.ring(0, n, self.src).start()
                self.ring(1, n, self.src).start()
            for n in range(TCH):
                self.mate(0, n, self.src, self.pr).start()

    def own(self, sem):
        return pltpu.make_async_copy(self.src.at[pl.ds(0, 1024)], self.out, sem)

    def step(self, who, chunks):
        @pl.when(who & ~self.root)
        def _():
            for n in chunks:
                self.ring(0, n, self.out).wait_recv()
                for k in range(4):
                    @pl.when(self.goes[k])
                    def _():
                        self.ring(k, n, self.out).start()

                @pl.when(self.z != 0)
                def _():
                    self.mate(self.core, n, self.out, self.pr).start()

    def finish(self):
        other, own = self.half(1 - self.core), self.half(self.core)
        me = self.z * 2 + self.core

        @pl.when(~self.root)
        def _():
            remote(other, other, self.ss.at[0], self.pr, prow=me).wait_recv()

        for k in range(4):
            @pl.when(self.goes[k])
            def _():
                remote(own, own, self.ss.at[k], self.pr, prow=me).wait_send()

        @pl.when(self.z != 0)
        def _():
            remote(own, own, self.ps.at[self.core], self.pr, prow=me).wait_send()

        @pl.when(self.root)
        def _():
            for half in range(2):
                ref = self.half(half)
                remote(ref, ref, self.ps.at[half], self.pr, prow=me).wait_send()


TOP_SEMS = [DMA((4,)), DMA((TCH,)), DMA((2,)), DMA]


def main_kernel(
    x_ref, pick_ref, panel_ref, linv_ref, uinv_ref, row_ref, extra_ref,
    m_ref, xm_ref, st_ref,
    slots, top, panel, panelf, wide, both, chosen, mask,
    zs, zr, zps, zpr, ts, tr, tps, tpr, ss, rs, last, sems,
):
    me = lax.axis_index("prow")
    ring = Ring(pick_ref, slots, zs, zr, zps, zpr)
    plane = Plane(panel_ref, panel, ss, rs, last)
    head = Top(x_ref, top, ts, tr, tps, tpr)
    row = row_ref[...]
    lanes = lax.broadcasted_iota(jnp.int32, (1, NB), 1)
    moved = row != lanes

    def swaps(b):
        rows = lax.broadcasted_iota(jnp.int32, (NB, NB), 0) + (b * NPROW + me) * NB
        hit = (rows == row) & moved
        m_ref[pl.ds(b * NB, NB), NB:] = onehot(hit, -1.0)
        gone = jnp.dot(onehot(hit), jnp.ones((NB, 128), BF), preferred_element_type=F32)
        for j in range(4):
            mask[pl.ds(j, NB, stride=4), :] = gone
        x = x_ref[pl.ds(b * 1024, 1024), :].astype(F32)
        xm_ref[pl.ds(b * 1024, 1024), :] = jnp.where(mask[...] > 0.5, 0.0, x).astype(BF)

    def lower(k):
        piece = panelf[pl.ds((k % 2) * 8 + k // 2, NB, stride=16), :].astype(BF)
        low = lax.dot_general(
            piece, uinv_ref[...], (((0,), (0,)), ((), ())), preferred_element_type=F32
        )
        m_ref[pl.ds(k * 128, 128), :NB] = low.astype(BF)

    greet(z_neighbours() + plane_neighbours())
    ring.begin()
    plane.begin()
    head.begin()
    q = lax.axis_index("pcol")
    own_panel = pltpu.make_async_copy(panel_ref, panel.at[pl.ds(q * 256, 256)], sems.at[0])
    own_panel.start()
    own_slot = pltpu.make_async_copy(pick_ref, ring.rows(ring.z, ring.core), sems.at[1])
    own_slot.start()

    @pl.when(head.root)
    def _():
        head.own(sems.at[2]).start()

    col = column_of(row)
    rank = ranks(row, col).astype(jnp.int32)
    ids = lax.broadcasted_iota(jnp.int32, (NB, 128), 0)
    lane = lax.broadcasted_iota(jnp.int32, (NB, 128), 1)
    goes = jnp.broadcast_to(col, (NB, 128)) != ids
    slot = jnp.where(
        goes & (rank < CAP), owner_of(jnp.broadcast_to(col, (NB, 128))) * CAP + rank, -1
    )
    stay = jnp.where(goes, -1, ids + NPROW * CAP)
    for u in range(WIDE // 128):
        hit = (slot == lane + 128 * u) | (stay == lane + 128 * u)
        chosen[:, 128 * u : 128 * (u + 1)] = onehot(hit)

    for b in range(8):
        swaps(b)

    near, middle, far = [
        head.relay & ((head.dist >= LEVEL[k]) & (head.dist < LEVEL[k + 1])) for k in range(3)
    ]
    first, second = range(TCH // 2), range(TCH // 2, TCH)
    ring.step(1)
    ring.step(2)
    plane.one()
    ring.step(3)
    plane.two()
    plane.three(0)
    head.step(near, first)
    ring.step(4)
    head.step(near, second)
    head.step(middle, first)
    plane.three(1)
    plane.three(2)
    ring.step(5)
    ring.step(6)
    head.step(middle, second)
    plane.three(3)
    head.step(far, range(TCH))
    plane.four()
    own_panel.wait()
    panelf[...] = panel[...].astype(F32)
    for k in range(16):
        lower(k)
    head.step(~head.relay, range(TCH))
    ring.step(7)
    ring.step(8)

    @pl.when(head.root)
    def _():
        head.own(sems.at[2]).wait()

    head.finish()
    plane.finish()
    wide[pl.ds(NPROW * SLOT, 1024), :] = top[...].astype(F32)
    for j in range(4):
        both[pl.ds(NPROW * CAP, NB), j * 128 : (j + 1) * 128] = wide[
            pl.ds(NPROW * SLOT + j, NB, stride=4), :
        ].astype(BF)
    st_ref[pl.ds(NB, NB), :] = both[pl.ds(NPROW * CAP, NB), :]
    own_slot.wait()
    ring.finish()
    wide[pl.ds(0, NPROW * SLOT), :] = slots[...].astype(F32)
    for j in range(4):
        both[pl.ds(0, NPROW * CAP), j * 128 : (j + 1) * 128] = wide[
            pl.ds(j, NPROW * CAP, stride=4), :
        ].astype(BF)
    picked = jnp.dot(chosen[...], both[...], preferred_element_type=F32)
    wide[pl.ds(0, 1024), :] = extra_ref[...].astype(F32)
    more = jnp.concatenate([wide[pl.ds(j, NB, stride=4), :] for j in range(4)], axis=1)
    picked = (picked + more).astype(BF)
    st_ref[pl.ds(0, NB), :] = jnp.dot(
        linv_ref[...], picked, preferred_element_type=F32
    ).astype(BF)


def main(tv, picked, pv, linv, uinv, row, extra):
    return pl.pallas_call(
        main_kernel,
        out_shape=(
            jax.ShapeDtypeStruct((8 * NB, 2 * NB), BF),
            jax.ShapeDtypeStruct((8192, 128), BF),
            jax.ShapeDtypeStruct((2 * NB, 2 * NB), BF),
        ),
        in_specs=[spec(VMEM)] * 7,
        out_specs=(spec(VMEM),) * 3,
        scratch_shapes=[
            VMEM((NPROW * SLOT, 128), BF),
            VMEM((1024, 128), BF),
            VMEM((4096, 128), BF),
            VMEM((4096, 128), F32),
            VMEM((4 * WIDE, 128), F32),
            VMEM((WIDE, 512), BF),
            VMEM((NB, WIDE), BF),
            VMEM((1024, 128), F32),
        ]
        + RING_SEMS
        + TOP_SEMS
        + [DMA, DMA((2, 12)), DMA]
        + [DMA((3,))],
        compiler_params=pltpu.CompilerParams(
            collective_id=0, has_side_effects=True, vmem_limit_bytes=40 * 2**20
        ),
        name="gather_prepare",
    )(tv, picked, pv, linv, uinv, row, extra)


def update_kernel(m_ref, xm_ref, st_ref, o_ref, spread, out, sem):
    copies = []
    for i in range(2048 // STEP):
        product = jnp.dot(m_ref[pl.ds(i * STEP, STEP), :], st_ref[...], preferred_element_type=F32)
        for j in range(4):
            spread[i % 2, pl.ds(j, STEP, stride=4), :] = product[:, j * 128 : (j + 1) * 128]
        at = pl.ds(i * STEP * 4, STEP * 4)
        out[at, :] = (xm_ref[at, :].astype(F32) - spread[i % 2]).astype(BF)
        if i == 0:
            @pl.when(lax.axis_index("prow") == 0)
            def _():
                for j in range(4):
                    solved = st_ref[pl.ds(0, NB), j * 128 : (j + 1) * 128]
                    spread[0, pl.ds(j, NB, stride=4), :] = solved.astype(F32)
                out[pl.ds(0, 4 * NB), :] = spread[0, pl.ds(0, 4 * NB), :].astype(BF)

        copies.append(pltpu.make_async_copy(out.at[at], o_ref.at[at], sem.at[i]))
        copies[-1].start()
    for c in copies:
        c.wait()


def update(m, xm, st):
    return pl.pallas_call(
        update_kernel,
        out_shape=jax.ShapeDtypeStruct((8192, 128), BF),
        in_specs=[spec(VMEM)] * 3,
        out_specs=spec(ANY),
        scratch_shapes=[
            VMEM((2, 4 * STEP, 128), F32), VMEM((8192, 128), BF), DMA((2048 // STEP,))
        ],
        compiler_params=pltpu.CompilerParams(vmem_limit_bytes=16 * 2**20),
        name="update",
    )(m, xm, st)


def per_device(trailing, panel, lower_inverse, upper_inverse, pivots):
    tv = trailing.reshape(8, 256, 2, 2, 128).transpose(0, 1, 3, 2, 4).reshape(8192, 128)
    pv = panel.reshape(16, 8, 2, 128).transpose(0, 2, 1, 3).reshape(256, 128)
    row = pivots.reshape(1, NB)
    picked, most = pick(trailing, row)
    extra = later_rounds(trailing, row, most)
    m, xm, st = main(tv, picked, pv, lower_inverse, upper_inverse, row, extra)
    out = update(m, xm, st)
    return out.reshape(8, 256, 2, 2, 128).transpose(0, 1, 3, 2, 4).reshape(trailing.shape)


def solution(mesh):
    placed = (P(None, "prow", None, "pcol"), P("pcol", None, "prow"), P(), P(), P())
    return jax.shard_map(
        per_device,
        mesh=mesh,
        in_specs=placed,
        out_specs=P(None, "prow", None, "pcol"),
        check_vma=False,
    )
```
